32 devices in a mesh: group: 2 (over x), seq: 16 (over z, y, core).
Axes of the slice: x: 2, y: 2, z: 4, core: 2. Of those that a mesh axis runs over, the one named last changes fastest.
Arguments:
- prefix_key: bfloat16 [4096, 2048], P(('group', 'seq')), parts along dimension 0, may hold values from -6 to 6
- prefix_value: bfloat16 [4096, 2048], P(('group', 'seq')), parts along dimension 0, may hold values from -6 to 6
- prefix_kappa: bfloat16 [4096, 2048], P(('group', 'seq')), parts along dimension 0, may hold values from -6 to 6
- prefix_decay: bfloat16 [4096, 2048], P(('group', 'seq')), parts along dimension 0, as said below
- prefix_learn: bfloat16 [4096, 2048], P(('group', 'seq')), parts along dimension 0, may hold values from 0.0049743652 to 0.049804688
- answer_query: bfloat16 [32, 4, 8, 2048], P(('group', 'seq')), parts along dimension 0, may hold values from -6 to 6
- answer_key: bfloat16 [32, 4, 8, 2048], P(('group', 'seq')), parts along dimension 0, may hold values from -6 to 6
- answer_value: bfloat16 [32, 4, 8, 2048], P(('group', 'seq')), parts along dimension 0, may hold values from -6 to 6
- answer_kappa: bfloat16 [32, 4, 8, 2048], P(('group', 'seq')), parts along dimension 0, may hold values from -6 to 6
- answer_decay: bfloat16 [32, 4, 8, 2048], P(('group', 'seq')), parts along dimension 0, as said below
- answer_learn: bfloat16 [32, 4, 8, 2048], P(('group', 'seq')), parts along dimension 0, may hold values from 0.0049743652 to 0.049804688
- doc_lengths: int32 [8], P('group'), parts along dimension 0, may hold values from 1 to 8, as said below
- question_doc: int32 [32], P(('group', 'seq')), parts along dimension 0, may hold values from 0 to 3
- choice_tokens: int32 [32, 4, 8], P(('group', 'seq')), parts along dimension 0, may hold values from 0 to 65535
- choice_lengths: int32 [32, 4], P(('group', 'seq')), parts along dimension 0, may hold values from 1 to 8, 20 in all within a row
- head_weight: bfloat16 [2048, 65536], P(None, 'seq')
Outputs:
- scores: float32 [32, 4], P(('group', 'seq')), parts along dimension 0
The draws below stay inside these ranges and needn't reach their ends.
There are 2 independent parts, one for each index of `group`. The reference program is written for one: setup_inputs(seed, part) draws one part's arguments, and reference() takes and returns one part's arrays. A program takes and returns all parts, laid end to end along the dimension named above; an argument that names none is the same for every part. Nothing has to cross between parts.
Inputs may be any that keep to these rules, and one draw needn't show every extreme that they name: `doc_lengths`: they sum to 16; the largest is exactly 8. `choice_lengths`: the lengths of one question's choices sum to 20, and the largest of them is exactly 8. `prefix_decay`: positive. `answer_decay`: positive.
All inputs are finite; a program needn't handle non-finite values.
Results may differ from the reference program's by a relative error of at most 0.0003.
The reference program's roundings to bfloat16 on the way (of `doc_state` and `hidden`) count: a program that leaves them out, or rounds other values in their place, can miss the bound.
Values may be sent and summed in bfloat16 or wider, within the bound.
A program may use at most 128 MiB of HBM per device.

```python
import math
import jax
import jax.numpy as jnp
import numpy as np
from jax import lax

HEADS = 32
HSIZE = 64
WIDTH = 2048
VOCAB = 65536
TOK_DEV = 128
QUEST_DEV = 1
CHOICES = 4
ANS_LEN = 8
QUESTIONS = 16
TOKENS = 2048
DOCS = 4
MOST_SPAN = 8
N_SEQ = 16


def rate_law(key, line_elements, block):
    attention_draw_seed, category_draw_seed, feature_draw_seed, segment_draw_seed, cluster_draw_seed = jax.random.split(key, 5)
    chain = float(MOST_SPAN * TOK_DEV)
    slow_low = math.log(0.1 / chain)
    slow_high = math.log(1.0 / chain)
    fast_share = 0.5
    head_pick = jax.random.uniform(attention_draw_seed, (HEADS,))
    slow_rate = jnp.exp(slow_low + (slow_high - slow_low) * head_pick)
    fast_rate = jnp.exp(math.log(1.0 / 50.0) + (math.log(1.0 / 30.0) - math.log(1.0 / 50.0)) * head_pick)
    fast_flag = jax.random.uniform(category_draw_seed, (HEADS,)) < fast_share
    head_rate = jnp.where(fast_flag, fast_rate, slow_rate)
    channel = jnp.exp(jax.random.uniform(feature_draw_seed, (line_elements, HEADS, HSIZE), minval=-0.7, maxval=0.7))
    blocks = line_elements // block
    shard_factor = jnp.exp(jax.random.uniform(segment_draw_seed, (blocks, 1, 1, 1), minval=-0.7, maxval=0.7))
    attribute_settings = head_rate[None, :, None] * channel
    attribute_settings = (attribute_settings.reshape(blocks, block, HEADS, HSIZE) * shard_factor).reshape(line_elements, HEADS, HSIZE)
    cluster_dispersion = jax.random.uniform(cluster_draw_seed, (line_elements, 1, 1)) < 4.0 / line_elements
    attribute_settings = attribute_settings + jnp.where(cluster_dispersion, 0.45, 0.0)
    return attribute_settings.reshape(line_elements, HEADS * HSIZE)


def draw_prefix_decay(key, part):
    line_elements = TOK_DEV * N_SEQ
    return rate_law(jax.random.fold_in(key, 11), line_elements, TOK_DEV).astype(jnp.bfloat16)


def draw_answer_decay(key, part):
    line_elements = QUEST_DEV * N_SEQ * CHOICES * ANS_LEN
    attribute_settings = rate_law(jax.random.fold_in(key, 23), line_elements, ANS_LEN)
    return attribute_settings.reshape(QUEST_DEV * N_SEQ, CHOICES, ANS_LEN, HEADS * HSIZE).astype(jnp.bfloat16)


def draw_doc_lengths(key, part):
    cut_seed, place_seed = jax.random.split(jax.random.fold_in(key, 53), 2)
    remainder = N_SEQ - MOST_SPAN
    candidates = jax.random.permutation(cut_seed, jnp.arange(1, remainder, dtype=jnp.int32))
    cuts = jnp.sort(candidates[:DOCS - 2])
    bounds = jnp.concatenate([jnp.zeros((1,), jnp.int32), cuts, jnp.full((1,), remainder, jnp.int32)])
    others = (bounds[1:] - bounds[:-1]).astype(jnp.int32)
    whole = jnp.concatenate([jnp.full((1,), MOST_SPAN, jnp.int32), others])
    offset = (jax.random.randint(place_seed, (), 0, DOCS) + part) % DOCS
    return jnp.roll(whole, offset).astype(jnp.int32)


def draw_head_weight(key, part):
    key_base = jax.random.fold_in(jax.random.fold_in(key, 37), 0)
    features = HEADS * HSIZE
    scale = 3.0 / math.sqrt(features)
    base = jax.random.normal(key_base, (features, VOCAB)) * scale
    return jnp.clip(base, -6.0 * scale, 6.0 * scale).astype(jnp.bfloat16)


def plant(entries, stream_key, least, largest):
    shape = entries.shape
    spot = [jax.random.randint(jax.random.fold_in(stream_key, axis), (), 0, shape[axis]) for axis in range(len(shape))]
    entries = entries.at[tuple(spot)].set(least)
    longest = shape.index(max(shape))
    spot[longest] = (spot[longest] + 1) % shape[longest]
    return entries.at[tuple(spot)].set(largest)


def block_scale(stream_key, dims, pieces, smallest, largest):
    gain, own = 1.0, jax.random.fold_in(stream_key, 6)
    for axis_at, shards_of in pieces:
        heights = jnp.exp(jax.random.uniform(jax.random.fold_in(own, axis_at), (shards_of,), jnp.float32, smallest / len(pieces), largest / len(pieces)))
        gain = gain * jnp.repeat(heights, dims[axis_at] // shards_of).reshape([-1 if axis == axis_at else 1 for axis in range(len(dims))])
    return gain


def cumulative_ranks(amount, slope):
    portions = [(1 << 20) // math.isqrt(rank ** slope) + 1 for rank in range(1, amount + 1)]
    deviation = 1 + sum(portions) // (1 << 30)
    return np.cumsum(np.array([max(1, weight // deviation) for weight in portions]))


def ranked(own_key, extent, number_of, skew):
    grid = cumulative_ranks(number_of, skew)
    lot = jax.random.randint(jax.random.fold_in(own_key, 1), extent, 0, int(grid[number_of - 1]))
    grade = jnp.searchsorted(jnp.asarray(grid, jnp.int32), lot, side="right")
    return jax.random.permutation(jax.random.fold_in(own_key, 2), number_of)[grade].astype(jnp.int32)


def profile(amount, total, bound, lean):
    loads = [(1 << 20) // math.isqrt(rank ** lean) + 1 for rank in range(2, amount + 1)]
    rest, counts = total - bound - (amount - 1), [1] * (amount - 1)
    while rest > 0:
        free = [i for i in range(amount - 1) if counts[i] < bound]
        mass, budget = sum([loads[i] for i in free]), rest
        for i in free:
            addition = min(bound - counts[i], max(1, budget * loads[i] // mass), rest)
            counts[i] = counts[i] + addition
            rest = rest - addition
    return np.array([bound] + counts)


def ragged_sizes(key, count, total, limit, skew):
    if count == 2:
        one = jax.random.randint(key, (), max(1, total - limit), min(limit, total - 1) + 1)
        return jnp.stack([one, total - one])
    tallies = jnp.asarray(profile(count, total, limit, skew), jnp.int32)
    pairs = (count - 1) // 2
    donor, sink = tallies[1:1 + 2 * pairs:2], tallies[2:2 + 2 * pairs:2]
    slack = jnp.minimum(donor - 1, limit - sink)
    passed = jax.random.randint(jax.random.fold_in(key, 1), (pairs,), 0, 1 << 20) % (slack + 1)
    tallies = tallies.at[1:1 + 2 * pairs:2].set(donor - passed).at[2:2 + 2 * pairs:2].set(sink + passed)
    return tallies[jax.random.permutation(jax.random.fold_in(key, 2), count)]


def bell_draw(own_key, extent, scale, most, shards=(), kind=jnp.bfloat16):
    factor_of = block_scale(own_key, extent, shards, -0.22, 0.18) if shards else 1.0
    values = jax.random.normal(own_key, extent, jnp.float32) * scale * factor_of
    return jnp.minimum(jnp.maximum(values, -most), most).astype(kind)


def setup_inputs(seed: int = 0, part: int = 0) -> dict:
    key_list = jax.random.split(jax.random.key(seed), 17)
    part_splits = jax.random.split(jax.random.fold_in(key_list[16], part), 17)
    prefix_key = bell_draw(part_splits[0], (TOKENS, WIDTH), 1.0, 6.0, ((0, 16),))
    prefix_value = bell_draw(part_splits[1], (TOKENS, WIDTH), 1.0, 6.0, ((0, 16),))
    prefix_kappa = bell_draw(part_splits[2], (TOKENS, WIDTH), 1.0, 6.0, ((0, 16),))
    prefix_decay = draw_prefix_decay(jax.random.fold_in(jax.random.fold_in(key_list[16], part), 71), part)
    prefix_learn = jnp.clip(jnp.exp(math.log(0.049804688) - 2.3038113 * jax.random.uniform(part_splits[4], (TOKENS, WIDTH), jnp.float32) ** block_scale(part_splits[4], (TOKENS, WIDTH), ((0, 16),), -0.2, 0.2)), 0.0049743652, 0.049804688).astype(jnp.bfloat16)
    answer_query = bell_draw(part_splits[5], (QUESTIONS, CHOICES, ANS_LEN, WIDTH), 1.0, 6.0, ((0, 16),))
    answer_key = bell_draw(part_splits[6], (QUESTIONS, CHOICES, ANS_LEN, WIDTH), 1.0, 6.0, ((0, 16),))
    answer_value = bell_draw(part_splits[7], (QUESTIONS, CHOICES, ANS_LEN, WIDTH), 1.0, 6.0, ((0, 16),))
    answer_kappa = bell_draw(part_splits[8], (QUESTIONS, CHOICES, ANS_LEN, WIDTH), 1.0, 6.0, ((0, 16),))
    answer_decay = draw_answer_decay(jax.random.fold_in(jax.random.fold_in(key_list[16], part), 71), part)
    answer_learn = jnp.clip(jnp.exp(math.log(0.049804688) - 2.3038113 * jax.random.uniform(part_splits[10], (QUESTIONS, CHOICES, ANS_LEN, WIDTH), jnp.float32) ** block_scale(part_splits[10], (QUESTIONS, CHOICES, ANS_LEN, WIDTH), ((0, 16),), -0.2, 0.2)), 0.0049743652, 0.049804688).astype(jnp.bfloat16)
    doc_lengths = draw_doc_lengths(jax.random.fold_in(jax.random.fold_in(key_list[16], part), 71), part)
    question_doc = plant(jax.random.randint(part_splits[12], (QUESTIONS,), 0, DOCS), jax.random.fold_in(part_splits[12], 1), 0, DOCS - 1).astype(jnp.int32)
    choice_tokens = plant(ranked(part_splits[13], (QUESTIONS, CHOICES, ANS_LEN), VOCAB, 2), jax.random.fold_in(part_splits[13], 3), 0, VOCAB - 1).astype(jnp.int32)
    choice_lengths = jax.vmap(lambda own: ragged_sizes(own, CHOICES, CHOICES * ANS_LEN * 5 // 8, ANS_LEN, 0))(jax.random.split(part_splits[14], QUESTIONS)).reshape((QUESTIONS, CHOICES)).astype(jnp.int32)
    head_weight = draw_head_weight(jax.random.fold_in(key_list[16], 71), part)
    return dict(prefix_key=prefix_key, prefix_value=prefix_value, prefix_kappa=prefix_kappa, prefix_decay=prefix_decay, prefix_learn=prefix_learn, answer_query=answer_query, answer_key=answer_key, answer_value=answer_value, answer_kappa=answer_kappa, answer_decay=answer_decay, answer_learn=answer_learn, doc_lengths=doc_lengths, question_doc=question_doc, choice_tokens=choice_tokens, choice_lengths=choice_lengths, head_weight=head_weight)


def split_heads(tensor):
    return tensor.astype(jnp.float32).reshape(tensor.shape[:-1] + (HEADS, HSIZE))

def transition(kappa, decay, learn):
    unit_kappa = kappa * lax.rsqrt(lax.optimization_barrier(jnp.sum(kappa * kappa, -1, keepdims=True)) + 1e-06)
    return (jnp.exp(-decay), unit_kappa, unit_kappa * learn)

def advance(memory, retain, unit_kappa, removal):
    projected = lax.optimization_barrier(jnp.sum(memory * unit_kappa[..., None, :], -1, keepdims=True))
    return memory * retain[..., None, :] - projected * removal[..., None, :]

def group_norm(values):
    centre = values - lax.optimization_barrier(jnp.mean(values, -1, keepdims=True))
    spread = lax.optimization_barrier(jnp.mean(centre * centre, -1, keepdims=True))
    return centre * lax.rsqrt(spread + 1e-05)

def reference(prefix_key, prefix_value, prefix_kappa, prefix_decay, prefix_learn, answer_query, answer_key, answer_value, answer_kappa, answer_decay, answer_learn, doc_lengths, question_doc, choice_tokens, choice_lengths, head_weight):
    doc_ends = jnp.cumsum(doc_lengths).astype(jnp.int32)
    doc_starts = (doc_ends - doc_lengths).astype(jnp.int32)
    shard_ids = jnp.arange(N_SEQ, dtype=jnp.int32)
    opened = jnp.any(doc_starts[None, :] == shard_ids[:, None], axis=1)

    def shaped(tensor):
        return tensor.reshape(N_SEQ, TOK_DEV, HEADS * HSIZE)

    def shard_step(memory, inputs):
        memory = jnp.where(inputs[0], jnp.float32(0.0), memory)

        def token_step(memory, token):
            key_now, value_now, kappa_now, decay_now, learn_now = [split_heads(tensor) for tensor in token]
            retain, unit_kappa, removal = transition(kappa_now, decay_now, learn_now)
            memory = advance(memory, retain, unit_kappa, removal) + value_now[:, :, None] * key_now[:, None, :]
            return (memory, None)
        memory, _ = lax.scan(token_step, memory, inputs[1:])
        return (memory, memory)
    start_memory = jnp.zeros((HEADS, HSIZE, HSIZE), jnp.float32)
    _, shard_end = lax.scan(shard_step, start_memory, (opened, shaped(prefix_key), shaped(prefix_value), shaped(prefix_kappa), shaped(prefix_decay), shaped(prefix_learn)))
    doc_state = shard_end[doc_ends - 1].astype(jnp.bfloat16)
    begin = doc_state[question_doc].astype(jnp.float32)
    memory = jnp.broadcast_to(begin[:, None], (QUESTIONS, CHOICES, HEADS, HSIZE, HSIZE))
    per_token = []
    for step in range(ANS_LEN):
        query_now = split_heads(answer_query[:, :, step])
        key_now = split_heads(answer_key[:, :, step])
        value_now = split_heads(answer_value[:, :, step])
        retain, unit_kappa, removal = transition(split_heads(answer_kappa[:, :, step]), split_heads(answer_decay[:, :, step]), split_heads(answer_learn[:, :, step]))
        memory = advance(memory, retain, unit_kappa, removal) + value_now[..., :, None] * key_now[..., None, :]
        per_token.append(lax.optimization_barrier(jnp.sum(memory * query_now[..., None, :], -1)))
    output = jnp.stack(per_token, 2)
    hidden = group_norm(output).reshape(QUESTIONS, CHOICES * ANS_LEN, HEADS * HSIZE).astype(jnp.bfloat16)

    def score_one(inputs):
        line_elements, targets = inputs
        logits = jnp.dot(line_elements, head_weight, preferred_element_type=jnp.float32)
        peak_logit = lax.optimization_barrier(jnp.max(logits, -1, keepdims=True))
        total = peak_logit[:, 0] + jnp.log(lax.optimization_barrier(jnp.sum(jnp.exp(logits - peak_logit), -1)))
        picked = jnp.take_along_axis(logits, targets[:, None], 1)[:, 0]
        return picked - total
    logprob = lax.map(score_one, (hidden, choice_tokens.reshape(QUESTIONS, CHOICES * ANS_LEN)))
    logprob = logprob.reshape(QUESTIONS, CHOICES, ANS_LEN)
    inside = jnp.arange(ANS_LEN, dtype=jnp.int32)[None, None, :] < choice_lengths[:, :, None]
    return lax.optimization_barrier(jnp.sum(jnp.where(inside, logprob, jnp.float32(0.0)), -1)) / choice_lengths.astype(jnp.float32)
```

```python
import functools

import jax
import jax.numpy as jnp
from jax import lax
from jax.experimental import pallas as pl
from jax.experimental.pallas import tpu as pltpu
from jax.sharding import PartitionSpec as P

HSIZE = 64
LANES = 128
WIDE = 256
CHUNK = 16
F32 = jnp.float32
BF16 = jnp.bfloat16


def split(x):
    high = x.astype(BF16)
    return high, (x - high.astype(F32)).astype(BF16)


def mm(a, b, dims):
    return lax.dot_general(a, b, (dims, ((), ())), preferred_element_type=F32)


NN = ((1,), (0,))
TN = ((0,), (0,))
NT = ((1,), (1,))


def dot3(a, b, dims=NN):
    ah, al = split(a)
    bh, bl = split(b)
    return mm(ah, bh, dims) + (mm(al, bh, dims) + mm(ah, bl, dims))


def block_mask(rows, cols):
    return (
        lax.broadcasted_iota(jnp.int32, (rows, cols), 0) // HSIZE
        == lax.broadcasted_iota(jnp.int32, (rows, cols), 1) // HSIZE
    )


def head_sum(x, ones):
    high, low = split(x)
    return mm(high, ones, NN) + mm(low, ones, NN)


def stack_heads(x):
    heads = x.shape[1] // HSIZE
    lane = lax.broadcasted_iota(jnp.int32, x.shape, 1) // HSIZE
    return jnp.concatenate([jnp.where(lane == h, x, jnp.zeros_like(x)) for h in range(heads)], 0)


def fold_heads(x):
    heads = x.shape[1] // HSIZE
    out = x[:HSIZE]
    for h in range(1, heads):
        out = out + x[h * HSIZE : (h + 1) * HSIZE]
    return out


def factors(kappa, decay, learn, ones):
    kappa = kappa.astype(F32)
    unit = kappa * lax.rsqrt(head_sum(kappa * kappa, ones) + 1e-06)
    return jnp.exp(-decay.astype(F32)), unit, unit * learn.astype(F32)


def prefix_group(key, value, kappa, decay, learn, ones, diag_block):
    rows, wide = key.shape
    chunks = rows // CHUNK
    retain, unit, removal = factors(kappa, decay, learn, ones)

    def halves(x):
        x = x.reshape(chunks, 2, 8, wide)
        return [x[:, 0], x[:, 1]]

    retain, unit, removal = halves(retain), halves(unit), halves(removal)
    sub = lax.broadcasted_iota(jnp.int32, (chunks, 8, wide), 1)

    def at(parts, step):
        return parts[step // 8][:, step % 8 : step % 8 + 1, :]

    def segments(x):
        return head_sum(x.reshape(chunks * 8, wide), ones).reshape(chunks, 8, wide)

    pushed = halves(key.astype(F32))
    for step in range(1, CHUNK):
        r, u, w = at(retain, step), at(unit, step), at(removal, step)
        for half in range(step // 8 + 1):
            if half * 8 >= step:
                continue
            x = pushed[half]
            new = x * r - segments(x * u) * w
            pushed[half] = new if step >= half * 8 + 8 else jnp.where(sub < step - half * 8, new, x)
    pulled = list(unit)
    for step in range(CHUNK - 2, -1, -1):
        r, u, w = at(retain, step), at(unit, step), at(removal, step)
        for half in range(2):
            if half * 8 + 7 <= step:
                continue
            x = pulled[half]
            new = x * r - segments(x * w) * u
            pulled[half] = new if step < half * 8 else jnp.where(sub > step - half * 8, new, x)
    tail = jnp.ones((chunks, 1, wide), F32)
    faded = [None] * CHUNK
    for step in range(CHUNK - 1, -1, -1):
        faded[step] = at(removal, step) * tail
        tail = tail * at(retain, step)

    def joined(parts):
        return jnp.concatenate([p.reshape(chunks, 1, 8, wide) for p in parts], 1).reshape(rows, wide)

    def spread(items):
        out = jnp.zeros((chunks, 8, wide), F32)
        for spot, item in enumerate(items):
            out = jnp.where(sub == spot, item, out)
        return out

    faded = joined([spread(faded[:8]), spread(faded[8:])])
    pulled = joined(pulled)
    pushed = joined(pushed)
    eye = lax.broadcasted_iota(jnp.int32, (wide, wide), 0) == lax.broadcasted_iota(
        jnp.int32, (wide, wide), 1
    )
    passage = None
    keys = None
    for c in range(chunks):
        part = slice(c * CHUNK, (c + 1) * CHUNK)
        low_rank = dot3(pulled[part], faded[part], TN)
        whole = jnp.where(eye, tail[c], 0.0) - jnp.where(diag_block, low_rank, 0.0)
        if c == 0:
            passage = fold_heads(whole)
            keys = pushed[part]
        else:
            moved = dot3(jnp.concatenate([passage, keys], 0), whole)
            passage = moved[:HSIZE]
            keys = jnp.concatenate([moved[HSIZE:], pushed[part]], 0)
    high, low = split(keys)
    outer = mm(value, high, TN) + mm(value, low, TN)
    return passage, fold_heads(jnp.where(diag_block, outer, 0.0))


def answer_group(query, key, value, kappa, decay, learn, ones):
    rows, wide = query.shape
    count = rows // 8
    retain, unit, removal = factors(kappa, decay, learn, ones)

    def tiled(x):
        return x.astype(F32).reshape(count, 8, wide)

    retain, unit, removal, key, value = [tiled(x) for x in (retain, unit, removal, key, value)]
    sub = lax.broadcasted_iota(jnp.int32, (count, 8, wide), 1)
    pulled = tiled(query)
    out = jnp.zeros_like(pulled)

    def segments(x):
        return head_sum(x.reshape(rows, wide), ones).reshape(count, 8, wide)

    for step in range(7, -1, -1):
        at = slice(step, step + 1)
        live = sub >= step
        out = out + jnp.where(live, segments(pulled * key[:, at]) * value[:, at], 0.0)
        new = pulled * retain[:, at] - segments(pulled * removal[:, at]) * unit[:, at]
        pulled = jnp.where(live, new, pulled)
    return pulled.reshape(rows, wide), out.reshape(rows, wide)


def states_kernel(*refs):
    pk, pv, pc, pd, pe, aq, ak, av, ac, ad, ae, moves, pulled, fresh = refs
    wide = WIDE
    diag_block = block_mask(wide, wide)
    ones = jnp.where(diag_block, 1.0, 0.0).astype(BF16)
    for g in range(pk.shape[1] // wide):
        s = slice(g * wide, (g + 1) * wide)
        passage, update = prefix_group(
            pk[:, s], pv[:, s], pc[:, s], pd[:, s], pe[:, s], ones, diag_block
        )
        for u in range(wide // LANES):
            lanes = slice(u * LANES, (u + 1) * LANES)
            moves[g * (wide // LANES) + u, :HSIZE] = passage[:, lanes]
            moves[g * (wide // LANES) + u, HSIZE:] = update[:, lanes]
        q, o = answer_group(aq[:, s], ak[:, s], av[:, s], ac[:, s], ad[:, s], ae[:, s], ones)
        pulled[:, s] = q
        fresh[:, s] = o


def chain_kernel(lengths, asked, moves, stage, states):
    shards = moves.shape[0]
    docs = lengths.shape[0]
    starts = []
    total = jnp.int32(0)
    for d in range(docs):
        starts.append(total)
        total = total + lengths[d]
    now = [None] * docs
    for d in range(docs):
        now[d] = moves[jnp.minimum(starts[d], shards - 1), HSIZE:]

    def step(j, now):
        out = []
        for d in range(docs):
            at = jnp.minimum(starts[d] + j, shards - 1)
            new = dot3(now[d], stack_heads(moves[at, :HSIZE])) + moves[at, HSIZE:]
            out.append(jnp.where(j < lengths[d], new, now[d]))
        return out

    now = lax.fori_loop(1, shards // 2, step, now)
    for d in range(docs):
        states[d] = now[d].astype(BF16)
    for q in range(shards):
        stage[q] = states[asked[q]]


def hidden_kernel(state, pulled, fresh, hidden):
    ones = jnp.where(block_mask(LANES, LANES), 1.0, 0.0).astype(BF16)
    for u in range(state.shape[0]):
        s = slice(u * LANES, (u + 1) * LANES)
        memory = stack_heads(state[u].astype(F32)).astype(BF16)
        x = pulled[:, s]
        high, low = split(x)
        lowest = (x - high.astype(F32) - low.astype(F32)).astype(BF16)
        out = mm(high, memory, NT) + (mm(low, memory, NT) + mm(lowest, memory, NT)) + fresh[:, s]
        centre = out - head_sum(out, ones) * (1.0 / HSIZE)
        spread = head_sum(centre * centre, ones) * (1.0 / HSIZE)
        hidden[:, s] = (centre * lax.rsqrt(spread + 1e-05)).astype(BF16)


def logits_kernel(offset, rows, ids, weight, stats, peak, mass, picked):
    step = pl.program_id(0)
    tile = weight.shape[1]

    @pl.when(step == 0)
    def _():
        peak[...] = jnp.full_like(peak, -jnp.inf)
        mass[...] = jnp.zeros_like(mass)
        picked[...] = jnp.zeros_like(picked)

    logits = jnp.dot(rows[...], weight[...], preferred_element_type=F32)
    column = lax.broadcasted_iota(jnp.int32, logits.shape, 1) + (offset[0] + step * tile)
    old = peak[:, :1]
    new = jnp.maximum(old, jnp.max(logits, 1, keepdims=True))
    add = jnp.sum(jnp.exp(logits - new), 1, keepdims=True)
    pick = jnp.sum(jnp.where(column == ids[:, :1], logits, 0.0), 1, keepdims=True)
    mass[...] = mass[...] * jnp.exp(old - new) + add
    picked[...] = picked[...] + pick
    peak[...] = jnp.broadcast_to(new, peak.shape)

    @pl.when(step == pl.num_programs(0) - 1)
    def _():
        lane = lax.broadcasted_iota(jnp.int32, stats.shape, 1)
        stats[...] = jnp.where(lane == 0, peak[...], jnp.where(lane == 1, mass[...], picked[...]))


VMEM = pl.BlockSpec(memory_space=pltpu.VMEM)
SMEM = pl.BlockSpec(memory_space=pltpu.SMEM)


def local(*args):
    prefix, answers = args[:5], args[5:11]
    doc_lengths, question_doc, choice_tokens, choice_lengths, head_weight = args[11:]
    shards = lax.axis_size("seq")
    my_index = lax.axis_index("seq")
    tok_rows, width = prefix[0].shape
    answers = [a.reshape(-1, width) for a in answers]
    rows = answers[0].shape[0]
    units = width // LANES
    copies = max(shards // units, 1)
    block = 2 * WIDE

    asked = lax.all_gather(question_doc, "seq", axis=0, tiled=True)
    part_ids = lax.all_gather(choice_tokens.reshape(-1), "seq", axis=0, tiled=True)

    moves, pulled, fresh = pl.pallas_call(
        states_kernel,
        grid=(width // block,),
        in_specs=[pl.BlockSpec((tok_rows, block), lambda i: (0, i))] * 5
        + [pl.BlockSpec((rows, block), lambda i: (0, i))] * 6,
        out_specs=[
            pl.BlockSpec((block // LANES, LANES, LANES), lambda i: (i, 0, 0)),
            pl.BlockSpec((rows, block), lambda i: (0, i)),
            pl.BlockSpec((rows, block), lambda i: (0, i)),
        ],
        out_shape=[
            jax.ShapeDtypeStruct((units, LANES, LANES), F32),
            jax.ShapeDtypeStruct((rows, width), F32),
            jax.ShapeDtypeStruct((rows, width), F32),
        ],
        compiler_params=pltpu.CompilerParams(vmem_limit_bytes=48 * 2**20),
        name="states",
    )(*prefix, *answers)
    if copies > 1:
        moves = jnp.repeat(moves, copies, axis=0)
    moves = lax.all_to_all(moves, "seq", split_axis=0, concat_axis=0, tiled=True)
    stage = pl.pallas_call(
        chain_kernel,
        in_specs=[SMEM, SMEM, VMEM],
        out_specs=VMEM,
        out_shape=jax.ShapeDtypeStruct((shards, HSIZE, LANES), BF16),
        scratch_shapes=[pltpu.VMEM((doc_lengths.shape[0], HSIZE, LANES), BF16)],
        name="chain",
    )(doc_lengths, asked, moves)
    state = lax.all_to_all(stage, "seq", split_axis=0, concat_axis=0, tiled=True)
    if copies > 1:
        state = state[::copies]
    hidden = pl.pallas_call(
        hidden_kernel,
        in_specs=[VMEM] * 3,
        out_specs=VMEM,
        out_shape=jax.ShapeDtypeStruct((rows, width), BF16),
        name="hidden",
    )(state, pulled, fresh)

    part_rows = lax.all_gather(hidden, "seq", axis=0, tiled=True)
    vocab_dev = head_weight.shape[1]
    tile = 512
    all_rows = shards * rows
    stats = pl.pallas_call(
        logits_kernel,
        grid=(vocab_dev // tile,),
        in_specs=[
            SMEM,
            pl.BlockSpec((all_rows, width), lambda i: (0, 0)),
            pl.BlockSpec((all_rows, LANES), lambda i: (0, 0)),
            pl.BlockSpec((width, tile), lambda i: (0, i)),
        ],
        out_specs=pl.BlockSpec((all_rows, LANES), lambda i: (0, 0)),
        out_shape=jax.ShapeDtypeStruct((all_rows, LANES), F32),
        scratch_shapes=[pltpu.VMEM((all_rows, LANES), F32)] * 3,
        compiler_params=pltpu.CompilerParams(vmem_limit_bytes=48 * 2**20),
        name="logits",
    )(
        (my_index * vocab_dev)[None],
        part_rows,
        jnp.broadcast_to(part_ids[:, None], (all_rows, LANES)),
        head_weight,
    )
    small = stats[:, :3].T.reshape(3, shards, rows).transpose(1, 0, 2)
    parts = lax.all_to_all(small, "seq", split_axis=0, concat_axis=0, tiled=True)
    peak, mass, picked = parts[:, 0], parts[:, 1], parts[:, 2]
    top = jnp.max(peak, 0)
    total = top + jnp.log(jnp.sum(mass * jnp.exp(peak - top[None, :]), 0))
    logprob = (jnp.sum(picked, 0) - total).reshape(choice_tokens.shape)
    inside = (
        jnp.arange(choice_tokens.shape[2], dtype=jnp.int32)[None, None, :]
        < choice_lengths[:, :, None]
    )
    return jnp.sum(jnp.where(inside, logprob, 0.0), -1) / choice_lengths.astype(F32)


def solution(mesh):
    token = P(("group", "seq"), None)
    choice = P(("group", "seq"), None, None, None)
    placed = (token,) * 5 + (choice,) * 6
    placed += (
        P("group"),
        P(("group", "seq")),
        P(("group", "seq"), None, None),
        P(("group", "seq"), None),
        P(None, "seq"),
    )
    return jax.shard_map(
        local, mesh=mesh, in_specs=placed, out_specs=P(("group", "seq"), None), check_vma=False
    )
```

```python
import functools

import jax
import jax.numpy as jnp
from jax import lax
from jax.experimental import pallas as pl
from jax.experimental.pallas import tpu as pltpu
from jax.sharding import PartitionSpec as P

HSIZE = 64
LANES = 128
WIDE = 256
CHUNK = 16
F32 = jnp.float32
BF16 = jnp.bfloat16


def split(x):
    high = x.astype(BF16)
    return high, (x - high.astype(F32)).astype(BF16)


def mm(a, b, dims):
    return lax.dot_general(a, b, (dims, ((), ())), preferred_element_type=F32)


NN = ((1,), (0,))
TN = ((0,), (0,))
NT = ((1,), (1,))


def dot3(a, b, dims=NN):
    ah, al = split(a)
    bh, bl = split(b)
    return mm(ah, bh, dims) + (mm(al, bh, dims) + mm(ah, bl, dims))


def block_mask(rows, cols):
    return (
        lax.broadcasted_iota(jnp.int32, (rows, cols), 0) // HSIZE
        == lax.broadcasted_iota(jnp.int32, (rows, cols), 1) // HSIZE
    )


def head_sum(x, ones):
    high, low = split(x)
    return mm(high, ones, NN) + mm(low, ones, NN)


def stack_heads(x):
    heads = x.shape[1] // HSIZE
    lane = lax.broadcasted_iota(jnp.int32, x.shape, 1) // HSIZE
    return jnp.concatenate([jnp.where(lane == h, x, jnp.zeros_like(x)) for h in range(heads)], 0)


def fold_heads(x):
    heads = x.shape[1] // HSIZE
    out = x[:HSIZE]
    for h in range(1, heads):
        out = out + x[h * HSIZE : (h + 1) * HSIZE]
    return out


def factors(kappa, decay, learn, ones):
    kappa = kappa.astype(F32)
    unit = kappa * lax.rsqrt(head_sum(kappa * kappa, ones) + 1e-06)
    return jnp.exp(-decay.astype(F32)), unit, unit * learn.astype(F32)


def prefix_group(key, value, kappa, decay, learn, ones, diag_block):
    rows, wide = key.shape
    chunks = rows // CHUNK
    retain, unit, removal = factors(kappa, decay, learn, ones)

    def halves(x):
        x = x.reshape(chunks, 2, 8, wide)
        return [x[:, 0], x[:, 1]]

    retain, unit, removal = halves(retain), halves(unit), halves(removal)
    sub = lax.broadcasted_iota(jnp.int32, (chunks, 8, wide), 1)

    def at(parts, step):
        return parts[step // 8][:, step % 8 : step % 8 + 1, :]

    def segments(x):
        return head_sum(x.reshape(chunks * 8, wide), ones).reshape(chunks, 8, wide)

    pushed = halves(key.astype(F32))
    for step in range(1, CHUNK):
        r, u, w = at(retain, step), at(unit, step), at(removal, step)
        for half in range(step // 8 + 1):
            if half * 8 >= step:
                continue
            x = pushed[half]
            new = x * r - segments(x * u) * w
            pushed[half] = new if step >= half * 8 + 8 else jnp.where(sub < step - half * 8, new, x)
    pulled = list(unit)
    for step in range(CHUNK - 2, -1, -1):
        r, u, w = at(retain, step), at(unit, step), at(removal, step)
        for half in range(2):
            if half * 8 + 7 <= step:
                continue
            x = pulled[half]
            new = x * r - segments(x * w) * u
            pulled[half] = new if step < half * 8 else jnp.where(sub > step - half * 8, new, x)
    tail = jnp.ones((chunks, 1, wide), F32)
    faded = [None] * CHUNK
    for step in range(CHUNK - 1, -1, -1):
        faded[step] = at(removal, step) * tail
        tail = tail * at(retain, step)

    def joined(parts):
        return jnp.concatenate([p.reshape(chunks, 1, 8, wide) for p in parts], 1).reshape(rows, wide)

    def spread(items):
        out = jnp.zeros((chunks, 8, wide), F32)
        for spot, item in enumerate(items):
            out = jnp.where(sub == spot, item, out)
        return out

    faded = joined([spread(faded[:8]), spread(faded[8:])])
    pulled = joined(pulled)
    pushed = joined(pushed)
    eye = lax.broadcasted_iota(jnp.int32, (wide, wide), 0) == lax.broadcasted_iota(
        jnp.int32, (wide, wide), 1
    )
    passage = None
    keys = None
    for c in range(chunks):
        part = slice(c * CHUNK, (c + 1) * CHUNK)
        low_rank = dot3(pulled[part], faded[part], TN)
        whole = jnp.where(eye, tail[c], 0.0) - jnp.where(diag_block, low_rank, 0.0)
        if c == 0:
            passage = fold_heads(whole)
            keys = pushed[part]
        else:
            moved = dot3(jnp.concatenate([passage, keys], 0), whole)
            passage = moved[:HSIZE]
            keys = jnp.concatenate([moved[HSIZE:], pushed[part]], 0)
    high, low = split(keys)
    outer = mm(value, high, TN) + mm(value, low, TN)
    return passage, fold_heads(jnp.where(diag_block, outer, 0.0))


def answer_group(query, key, value, kappa, decay, learn, ones):
    rows, wide = query.shape
    count = rows // 8
    retain, unit, removal = factors(kappa, decay, learn, ones)

    def tiled(x):
        return x.astype(F32).reshape(count, 8, wide)

    retain, unit, removal, key, value = [tiled(x) for x in (retain, unit, removal, key, value)]
    sub = lax.broadcasted_iota(jnp.int32, (count, 8, wide), 1)
    pulled = tiled(query)
    out = jnp.zeros_like(pulled)

    def segments(x):
        return head_sum(x.reshape(rows, wide), ones).reshape(count, 8, wide)

    for step in range(7, -1, -1):
        at = slice(step, step + 1)
        live = sub >= step
        out = out + jnp.where(live, segments(pulled * key[:, at]) * value[:, at], 0.0)
        new = pulled * retain[:, at] - segments(pulled * removal[:, at]) * unit[:, at]
        pulled = jnp.where(live, new, pulled)
    return pulled.reshape(rows, wide), out.reshape(rows, wide)


def states_kernel(*refs):
    pk, pv, pc, pd, pe, aq, ak, av, ac, ad, ae, moves, pulled, fresh = refs
    wide = WIDE
    diag_block = block_mask(wide, wide)
    ones = jnp.where(diag_block, 1.0, 0.0).astype(BF16)
    for g in range(pk.shape[1] // wide):
        s = slice(g * wide, (g + 1) * wide)
        passage, update = prefix_group(
            pk[:, s], pv[:, s], pc[:, s], pd[:, s], pe[:, s], ones, diag_block
        )
        for u in range(wide // LANES):
            lanes = slice(u * LANES, (u + 1) * LANES)
            moves[g * (wide // LANES) + u, :HSIZE] = passage[:, lanes]
            moves[g * (wide // LANES) + u, HSIZE:] = update[:, lanes]
        q, o = answer_group(aq[:, s], ak[:, s], av[:, s], ac[:, s], ad[:, s], ae[:, s], ones)
        pulled[:, s] = q
        fresh[:, s] = o


def documents(lengths, moves):
    shards = moves.shape[0]
    docs = lengths.shape[0]
    starts = []
    total = jnp.int32(0)
    for d in range(docs):
        starts.append(total)
        total = total + lengths[d]
    now = [moves[jnp.minimum(starts[d], shards - 1), HSIZE:] for d in range(docs)]

    def step(j, now):
        out = []
        for d in range(docs):
            at = jnp.minimum(starts[d] + j, shards - 1)
            new = dot3(now[d], stack_heads(moves[at, :HSIZE])) + moves[at, HSIZE:]
            out.append(jnp.where(j < lengths[d], new, now[d]))
        return out

    return [x.astype(BF16) for x in lax.fori_loop(1, shards // 2, step, now)]


def hidden_unit(state, x, fresh, ones):
    memory = stack_heads(state.astype(F32)).astype(BF16)
    high, low = split(x)
    lowest = (x - high.astype(F32) - low.astype(F32)).astype(BF16)
    out = mm(high, memory, NT) + (mm(low, memory, NT) + mm(lowest, memory, NT)) + fresh
    centre = out - head_sum(out, ones) * (1.0 / HSIZE)
    spread = head_sum(centre * centre, ones) * (1.0 / HSIZE)
    return (centre * lax.rsqrt(spread + 1e-05)).astype(BF16)


def score_kernel(
    copies,
    lengths,
    choice_lengths,
    meta,
    moves,
    pulled,
    fresh,
    weight,
    scores,
    meta_all,
    moves_all,
    stage,
    state,
    rows_all,
    weight_all,
    stats,
    stats_all,
    peak,
    mass,
    picked,
    weight_sem,
    meta_send,
    meta_recv,
    move_send,
    move_recv,
    state_send,
    state_recv,
    far_send,
    far_recv,
    mid_send,
    mid_recv,
    near_send,
    near_recv,
    stat_send,
    stat_recv,
):
    shards = moves_all.shape[0]
    me = lax.axis_index("seq")
    rows = pulled.shape[0]
    tiles, _, tile = weight_all.shape

    def fetch(i):
        return pltpu.make_async_copy(
            weight.at[:, pl.ds(i * tile, tile)], weight_all.at[i], weight_sem.at[i]
        )

    for i in range(tiles):
        fetch(i).start()

    def send(source, target, send_sem, recv_sem, dest):
        copy = pltpu.make_async_remote_copy(
            src_ref=source,
            dst_ref=target,
            send_sem=send_sem,
            recv_sem=recv_sem,
            device_id={"seq": dest},
            device_id_type=pl.DeviceIdType.MESH,
        )
        copy.start()
        return copy

    barrier = pltpu.get_barrier_semaphore()
    for k in range(1, shards):
        pl.semaphore_signal(
            barrier,
            inc=1,
            device_id={"seq": lax.rem(me + k, shards)},
            device_id_type=pl.DeviceIdType.MESH,
        )
    pl.semaphore_wait(barrier, shards - 1)

    sent = []
    arriving = []
    for k in range(1, shards):
        dest = lax.rem(me + k, shards)
        small = send(meta, meta_all.at[me], meta_send.at[k], meta_recv.at[k], dest)
        large = send(
            moves.at[dest // copies], moves_all.at[me], move_send.at[k], move_recv.at[k], dest
        )
        arriving += [small, large]
    meta_all[me] = meta[...]
    moves_all[me] = moves[me // copies]
    for copy in arriving:
        copy.wait_recv()
    sent += arriving

    docs = documents(lengths, moves_all)
    for q in range(shards):
        asked = jnp.broadcast_to(meta_all[q, rows : rows + 1, :], docs[0].shape)
        chosen = docs[0].astype(F32)
        for d in range(1, len(docs)):
            chosen = jnp.where(asked == d, docs[d].astype(F32), chosen)
        stage[q] = chosen.astype(BF16)
    unit = me // copies
    arriving = []
    for k in range(copies, shards, copies):
        dest = lax.rem(me + k, shards)
        arriving.append(
            send(stage.at[dest], state.at[unit], state_send.at[k], state_recv.at[k], dest)
        )
    state[unit] = stage[me]
    for copy in arriving:
        copy.wait_recv()
    sent += arriving

    ones = jnp.where(block_mask(LANES, LANES), 1.0, 0.0).astype(BF16)
    for u in range(state.shape[0]):
        s = slice(u * LANES, (u + 1) * LANES)
        rows_all[me, :, s] = hidden_unit(state[u], pulled[:, s], fresh[:, s], ones)

    hops = shards // 4
    far, place = me // 4, lax.rem(me, 4)
    mid_peer = me + 2 - 4 * (place // 2)
    near_peer = me + 1 - 2 * lax.rem(me, 2)

    def pass_on(slot, send_sems, recv_sems, k, dest):
        return send(rows_all.at[slot], rows_all.at[slot], send_sems.at[k], recv_sems.at[k], dest)

    fars = [None]
    for d in range(1, hops):
        dest = lax.rem(far + d, hops) * 4 + place
        fars.append(pass_on(me, far_send, far_recv, d, dest))
    mids = [pass_on(me, mid_send, mid_recv, 0, mid_peer)]
    nears = [pass_on(me, near_send, near_recv, 0, near_peer)]
    later = []

    def from_mid(d):
        mids[d].wait_recv()
        slot = lax.rem(far - d + hops, hops) * 4 + lax.rem(place + 2, 4)
        later.append(pass_on(slot, near_send, near_recv, hops + d, near_peer))

    for d in range(1, hops):
        fars[d].wait_recv()
        slot = lax.rem(far - d + hops, hops) * 4 + place
        mids.append(pass_on(slot, mid_send, mid_recv, d, mid_peer))
        nears.append(pass_on(slot, near_send, near_recv, d, near_peer))
        from_mid(d - 1)
    from_mid(hops - 1)
    for copy in nears + later:
        copy.wait_recv()
    sent += fars[1:] + mids + nears + later

    total = shards * rows
    peak[...] = jnp.full_like(peak, -jnp.inf)
    mass[...] = jnp.zeros_like(mass)
    picked[...] = jnp.zeros_like(picked)
    first = me * (tiles * tile)

    def score_tile(i, carry):
        fetch(i).wait()
        everyone = rows_all[...].reshape(total, rows_all.shape[2])
        logits = jnp.dot(everyone, weight_all[i], preferred_element_type=F32)
        ids = meta_all[:, :rows, :].reshape(total, LANES)
        parts = [logits[:, p * LANES : (p + 1) * LANES] for p in range(tile // LANES)]
        old = peak[...]
        new = functools.reduce(jnp.maximum, parts, old)
        add = mass[...] * jnp.exp(old - new)
        pick = picked[...]
        lane = lax.broadcasted_iota(jnp.int32, (total, LANES), 1) - ids
        for p, part in enumerate(parts):
            add = add + jnp.exp(part - new)
            pick = pick + jnp.where(lane == -(first + i * tile + p * LANES), part, 0.0)
        peak[...] = new
        mass[...] = add
        picked[...] = pick
        return carry

    lax.fori_loop(0, tiles, score_tile, 0)
    top = jnp.max(peak[...], 1, keepdims=True)
    summed = jnp.sum(mass[...] * jnp.exp(peak[...] - top), 1, keepdims=True)
    chosen = jnp.sum(picked[...], 1, keepdims=True)
    lane = lax.broadcasted_iota(jnp.int32, (total, LANES), 1)
    packed = jnp.where(lane == 0, top, jnp.where(lane == 1, summed, chosen))
    stats[...] = packed.reshape(shards, rows, LANES)

    arriving = []
    for k in range(1, shards):
        dest = lax.rem(me + k, shards)
        arriving.append(
            send(stats.at[dest], stats_all.at[me], stat_send.at[k], stat_recv.at[k], dest)
        )
    stats_all[me] = stats[me]
    for copy in arriving:
        copy.wait_recv()
    sent += arriving
    tops = stats_all[:, :, 0:1]
    overall = jnp.max(tops, 0)
    masses = jnp.sum(stats_all[:, :, 1:2] * jnp.exp(tops - overall[None]), 0)
    logprob = jnp.sum(stats_all[:, :, 2:3], 0) - (overall + jnp.log(masses))
    logprob = jnp.broadcast_to(logprob, (rows, LANES))
    slots = rows // choice_lengths.shape[1]
    spot = lax.broadcasted_iota(jnp.int32, (slots, LANES), 0)
    for c in range(choice_lengths.shape[1]):
        count = choice_lengths[0, c]
        mine = jnp.where(spot < count, logprob[c * slots : (c + 1) * slots], 0.0)
        scores[c : c + 1, :] = jnp.sum(mine, 0, keepdims=True) / jnp.full(
            (1, LANES), count, jnp.int32
        ).astype(F32)
    for copy in sent:
        copy.wait_send()


VMEM = pl.BlockSpec(memory_space=pltpu.VMEM)
SMEM = pl.BlockSpec(memory_space=pltpu.SMEM)


def local(*args):
    prefix, answers = args[:5], args[5:11]
    doc_lengths, question_doc, choice_tokens, choice_lengths, head_weight = args[11:]
    shards = lax.axis_size("seq")
    my_index = lax.axis_index("seq")
    tok_rows, width = prefix[0].shape
    answers = [a.reshape(-1, width) for a in answers]
    rows = answers[0].shape[0]
    units = width // LANES
    copies = max(shards // units, 1)
    block = 2 * WIDE

    moves, pulled, fresh = pl.pallas_call(
        states_kernel,
        grid=(width // block,),
        in_specs=[pl.BlockSpec((tok_rows, block), lambda i: (0, i))] * 5
        + [pl.BlockSpec((rows, block), lambda i: (0, i))] * 6,
        out_specs=[
            pl.BlockSpec((block // LANES, LANES, LANES), lambda i: (i, 0, 0)),
            pl.BlockSpec((rows, block), lambda i: (0, i)),
            pl.BlockSpec((rows, block), lambda i: (0, i)),
        ],
        out_shape=[
            jax.ShapeDtypeStruct((units, LANES, LANES), F32),
            jax.ShapeDtypeStruct((rows, width), F32),
            jax.ShapeDtypeStruct((rows, width), F32),
        ],
        compiler_params=pltpu.CompilerParams(vmem_limit_bytes=60 * 2**20),
        name="states",
    )(*prefix, *answers)
    meta = jnp.concatenate(
        [choice_tokens.reshape(-1), jnp.broadcast_to(question_doc, (8,))]
    )
    meta = jnp.broadcast_to(meta[:, None], (rows + 8, LANES))
    vocab_dev = head_weight.shape[1]
    tile = 512
    all_rows = shards * rows
    choices = choice_tokens.shape[1]
    dma = pltpu.SemaphoreType.DMA
    scores = pl.pallas_call(
        functools.partial(score_kernel, copies),
        in_specs=[SMEM, SMEM, VMEM, VMEM, VMEM, VMEM, pl.BlockSpec(memory_space=pl.ANY)],
        out_specs=VMEM,
        out_shape=jax.ShapeDtypeStruct((choices, LANES), F32),
        scratch_shapes=[
            pltpu.VMEM((shards, rows + 8, LANES), jnp.int32),
            pltpu.VMEM((shards, LANES, LANES), F32),
            pltpu.VMEM((shards, HSIZE, LANES), BF16),
            pltpu.VMEM((units, HSIZE, LANES), BF16),
            pltpu.VMEM((shards, rows, width), BF16),
            pltpu.VMEM((vocab_dev // tile, width, tile), BF16),
            pltpu.VMEM((shards, rows, LANES), F32),
            pltpu.VMEM((shards, rows, LANES), F32),
            pltpu.VMEM((all_rows, LANES), F32),
            pltpu.VMEM((all_rows, LANES), F32),
            pltpu.VMEM((all_rows, LANES), F32),
            dma((vocab_dev // tile,)),
        ]
        + [dma((shards,))] * 14,
        compiler_params=pltpu.CompilerParams(
            vmem_limit_bytes=60 * 2**20, collective_id=0, has_side_effects=True
        ),
        name="score",
    )(doc_lengths, choice_lengths, meta, moves, pulled, fresh, head_weight)
    return scores[:, 0][None]


def solution(mesh):
    token = P(("group", "seq"), None)
    choice = P(("group", "seq"), None, None, None)
    placed = (token,) * 5 + (choice,) * 6
    placed += (
        P("group"),
        P(("group", "seq")),
        P(("group", "seq"), None, None),
        P(("group", "seq"), None),
        P(None, "seq"),
    )
    return jax.shard_map(
        local, mesh=mesh, in_specs=placed, out_specs=P(("group", "seq"), None), check_vma=False
    )
```

```python
import functools

import jax
import jax.numpy as jnp
from jax import lax
from jax.experimental import pallas as pl
from jax.experimental.pallas import tpu as pltpu
from jax.sharding import PartitionSpec as P

HSIZE = 64
LANES = 128
WIDE = 256
F32 = jnp.float32
BF16 = jnp.bfloat16


def split(x):
    high = x.astype(BF16)
    return high, (x - high.astype(F32)).astype(BF16)


def mm(a, b, dims):
    return lax.dot_general(a, b, (dims, ((), ())), preferred_element_type=F32)


NN = ((1,), (0,))
TN = ((0,), (0,))
NT = ((1,), (1,))


def dot3(a, b, dims=NN):
    ah, al = split(a)
    bh, bl = split(b)
    rows = a.shape[0]
    if dims != TN and rows % 16 == 0:
        both = mm(jnp.concatenate([ah, al], 0), bh, dims)
        return both[:rows] + (both[rows:] + mm(ah, bl, dims))
    return mm(ah, bh, dims) + (mm(al, bh, dims) + mm(ah, bl, dims))


def block_mask(rows, cols):
    return (
        lax.broadcasted_iota(jnp.int32, (rows, cols), 0) // HSIZE
        == lax.broadcasted_iota(jnp.int32, (rows, cols), 1) // HSIZE
    )


def head_sum(x, ones):
    rows = x.shape[0]
    high, low = split(x)
    both = mm(jnp.concatenate([high, low], 0), ones, NN)
    return both[:rows] + both[rows:]


def stack_heads(x):
    heads = x.shape[1] // HSIZE
    lane = lax.broadcasted_iota(jnp.int32, x.shape, 1) // HSIZE
    return jnp.concatenate([jnp.where(lane == h, x, jnp.zeros_like(x)) for h in range(heads)], 0)


def fold_heads(x):
    heads = x.shape[1] // HSIZE
    out = x[:HSIZE]
    for h in range(1, heads):
        out = out + x[h * HSIZE : (h + 1) * HSIZE]
    return out


def factors(kappa, decay, learn, ones):
    kappa = kappa.astype(F32)
    unit = kappa * lax.rsqrt(head_sum(kappa * kappa, ones) + 1e-06)
    return jnp.exp(-decay.astype(F32)), unit, unit * learn.astype(F32)


def merge(first, second):
    gain_a, pulled_a, faded_a, keys_a = first
    gain_b, pulled_b, faded_b, keys_b = second
    seen = dot3(pulled_b, stack_heads(faded_a), NT)
    moved = gain_a * pulled_b - dot3(seen, stack_heads(pulled_a))
    hit = dot3(keys_a, stack_heads(pulled_b), NT)
    kept = gain_b * keys_a - dot3(hit, stack_heads(faded_b))
    return (
        gain_a * gain_b,
        jnp.concatenate([pulled_a, moved], 0),
        jnp.concatenate([gain_b * faded_a, faded_b], 0),
        jnp.concatenate([kept, keys_b], 0),
    )


def state_group(prefix, answers, ones, diag_block):
    key, value, kappa, decay, learn = prefix
    query, akey, avalue, akappa, adecay, alearn = answers
    rows, wide = key.shape
    arows = query.shape[0]
    retain, unit, removal = factors(
        jnp.concatenate([kappa, akappa], 0),
        jnp.concatenate([decay, adecay], 0),
        jnp.concatenate([learn, alearn], 0),
        ones,
    )

    def tiled(x):
        return x.reshape(-1, 8, wide)

    tiles = rows // 8
    aretain, aunit, aremoval = [tiled(x[rows:]) for x in (retain, unit, removal)]
    retain, unit, removal = [tiled(x[:rows]) for x in (retain, unit, removal)]
    akey, avalue = tiled(akey.astype(F32)), tiled(avalue.astype(F32))
    sub = lax.broadcasted_iota(jnp.int32, (tiles, 8, wide), 1)
    asub = sub[: arows // 8]
    pushed = tiled(key.astype(F32))
    pulled = unit
    apulled = tiled(query.astype(F32))
    out = jnp.zeros_like(apulled)
    for t in range(8):
        j = 7 - t
        pt = slice(t, t + 1)
        aj = slice(j, j + 1)
        terms = [apulled * akey[:, aj], apulled * aremoval[:, aj]]
        if t == 0:
            terms = [x.reshape(-1, wide) for x in terms]
            sums = head_sum(jnp.concatenate(terms, 0), ones)
            got, gone = tiled(sums[:arows]), tiled(sums[arows:])
        if t > 0:
            pj = slice(7 - t, 8 - t)
            terms = [pushed * unit[:, pt], pulled * removal[:, pj]] + terms
            terms = [x.reshape(-1, wide) for x in terms]
            sums = head_sum(jnp.concatenate(terms, 0), ones)
            new = pushed * retain[:, pt] - tiled(sums[:rows]) * removal[:, pt]
            pushed = jnp.where(sub < t, new, pushed)
            new = pulled * retain[:, pj] - tiled(sums[rows : 2 * rows]) * unit[:, pj]
            pulled = jnp.where(sub > 7 - t, new, pulled)
            got = tiled(sums[2 * rows : 2 * rows + arows])
            gone = tiled(sums[2 * rows + arows :])
        live = asub >= j
        out = out + jnp.where(live, got * avalue[:, aj], 0.0)
        apulled = jnp.where(live, apulled * aretain[:, aj] - gone * aunit[:, aj], apulled)
    gain = jnp.ones((tiles, 1, wide), F32)
    faded = removal
    for t in range(7, -1, -1):
        faded = jnp.where(sub == t, removal * gain, faded)
        gain = gain * retain[:, t : t + 1]
    parts = [(gain[c], pulled[c], faded[c], pushed[c]) for c in range(tiles)]
    while len(parts) > 1:
        parts = [merge(parts[i], parts[i + 1]) for i in range(0, len(parts), 2)]
    gain, pulled, faded, keys = parts[0]
    low_rank = fold_heads(jnp.where(diag_block, dot3(pulled, faded, TN), 0.0))
    eye = (
        lax.broadcasted_iota(jnp.int32, (HSIZE, wide), 0)
        == lax.broadcasted_iota(jnp.int32, (HSIZE, wide), 1) % HSIZE
    )
    passage = jnp.where(eye, gain, 0.0) - low_rank
    high, low = split(keys)
    outer = mm(value, high, TN) + mm(value, low, TN)
    update = fold_heads(jnp.where(diag_block, outer, 0.0))
    return passage, update, apulled.reshape(arows, wide), out.reshape(arows, wide)


def states_kernel(*refs):
    pk, pv, pc, pd, pe, aq, ak, av, ac, ad, ae, moves, pulled, fresh = refs
    wide = WIDE
    diag_block = block_mask(wide, wide)
    ones = jnp.where(diag_block, 1.0, 0.0).astype(BF16)
    for g in range(pk.shape[1] // wide):
        s = slice(g * wide, (g + 1) * wide)
        passage, update, q, o = state_group(
            [r[:, s] for r in (pk, pv, pc, pd, pe)],
            [r[:, s] for r in (aq, ak, av, ac, ad, ae)],
            ones,
            diag_block,
        )
        for u in range(wide // LANES):
            lanes = slice(u * LANES, (u + 1) * LANES)
            moves[g * (wide // LANES) + u, :HSIZE] = passage[:, lanes]
            moves[g * (wide // LANES) + u, HSIZE:] = update[:, lanes]
        pulled[:, s] = q
        fresh[:, s] = o


def documents(lengths, moves):
    shards = moves.shape[0]
    docs = lengths.shape[0]
    starts = []
    total = jnp.int32(0)
    for d in range(docs):
        starts.append(total)
        total = total + lengths[d]
    now = [moves[jnp.minimum(starts[d], shards - 1), HSIZE:] for d in range(docs)]

    def step(j, now):
        out = []
        for d in range(docs):
            at = jnp.minimum(starts[d] + j, shards - 1)
            new = dot3(now[d], stack_heads(moves[at, :HSIZE])) + moves[at, HSIZE:]
            out.append(jnp.where(j < lengths[d], new, now[d]))
        return out

    return [x.astype(BF16) for x in lax.fori_loop(1, shards // 2, step, now)]


def hidden_unit(state, x, fresh, ones):
    memory = stack_heads(state.astype(F32)).astype(BF16)
    high, low = split(x)
    lowest = (x - high.astype(F32) - low.astype(F32)).astype(BF16)
    out = mm(high, memory, NT) + (mm(low, memory, NT) + mm(lowest, memory, NT)) + fresh
    centre = out - head_sum(out, ones) * (1.0 / HSIZE)
    spread = head_sum(centre * centre, ones) * (1.0 / HSIZE)
    return (centre * lax.rsqrt(spread + 1e-05)).astype(BF16)


def score_kernel(
    copies,
    lengths,
    choice_lengths,
    meta,
    moves,
    pulled,
    fresh,
    weight,
    scores,
    meta_all,
    moves_all,
    stage,
    state,
    rows_all,
    weight_all,
    stats,
    stats_all,
    peak,
    mass,
    picked,
    weight_sem,
    meta_send,
    meta_recv,
    move_send,
    move_recv,
    state_send,
    state_recv,
    far_send,
    far_recv,
    mid_send,
    mid_recv,
    near_send,
    near_recv,
    stat_send,
    stat_recv,
):
    shards = moves_all.shape[0]
    me = lax.axis_index("seq")
    rows = pulled.shape[0]
    tiles, _, tile = weight_all.shape

    def fetch(i):
        return pltpu.make_async_copy(
            weight.at[:, pl.ds(i * tile, tile)], weight_all.at[i], weight_sem.at[i]
        )

    for i in range(tiles):
        fetch(i).start()

    def send(source, target, send_sem, recv_sem, dest):
        copy = pltpu.make_async_remote_copy(
            src_ref=source,
            dst_ref=target,
            send_sem=send_sem,
            recv_sem=recv_sem,
            device_id={"seq": dest},
            device_id_type=pl.DeviceIdType.MESH,
        )
        copy.start()
        return copy

    barrier = pltpu.get_barrier_semaphore()
    for k in range(1, shards):
        pl.semaphore_signal(
            barrier,
            inc=1,
            device_id={"seq": lax.rem(me + k, shards)},
            device_id_type=pl.DeviceIdType.MESH,
        )
    pl.semaphore_wait(barrier, shards - 1)

    sent = []
    arriving = []
    for k in range(1, shards):
        dest = lax.rem(me + k, shards)
        small = send(meta, meta_all.at[me], meta_send.at[k], meta_recv.at[k], dest)
        large = send(
            moves.at[dest // copies], moves_all.at[me], move_send.at[k], move_recv.at[k], dest
        )
        arriving += [small, large]
    meta_all[me] = meta[...]
    moves_all[me] = moves[me // copies]
    for copy in arriving:
        copy.wait_recv()
    sent += arriving

    docs = documents(lengths, moves_all)
    for q in range(shards):
        asked = jnp.broadcast_to(meta_all[q, rows : rows + 1, :], docs[0].shape)
        chosen = docs[0].astype(F32)
        for d in range(1, len(docs)):
            chosen = jnp.where(asked == d, docs[d].astype(F32), chosen)
        stage[q] = chosen.astype(BF16)
    unit = me // copies
    arriving = []
    for k in range(copies, shards, copies):
        dest = lax.rem(me + k, shards)
        arriving.append(
            send(stage.at[dest], state.at[unit], state_send.at[k], state_recv.at[k], dest)
        )
    state[unit] = stage[me]
    for copy in arriving:
        copy.wait_recv()
    sent += arriving

    ones = jnp.where(block_mask(LANES, LANES), 1.0, 0.0).astype(BF16)
    for u in range(state.shape[0]):
        s = slice(u * LANES, (u + 1) * LANES)
        rows_all[me, :, s] = hidden_unit(state[u], pulled[:, s], fresh[:, s], ones)

    hops = shards // 4
    far, place = me // 4, lax.rem(me, 4)
    mid_peer = me + 2 - 4 * (place // 2)
    near_peer = me + 1 - 2 * lax.rem(me, 2)

    def pass_on(slot, send_sems, recv_sems, k, dest):
        return send(rows_all.at[slot], rows_all.at[slot], send_sems.at[k], recv_sems.at[k], dest)

    fars = [None]
    for d in range(1, hops):
        dest = lax.rem(far + d, hops) * 4 + place
        fars.append(pass_on(me, far_send, far_recv, d, dest))
    mids = [pass_on(me, mid_send, mid_recv, 0, mid_peer)]
    nears = [pass_on(me, near_send, near_recv, 0, near_peer)]
    later = []

    def from_mid(d):
        mids[d].wait_recv()
        slot = lax.rem(far - d + hops, hops) * 4 + lax.rem(place + 2, 4)
        later.append(pass_on(slot, near_send, near_recv, hops + d, near_peer))

    for d in range(1, hops):
        fars[d].wait_recv()
        slot = lax.rem(far - d + hops, hops) * 4 + place
        mids.append(pass_on(slot, mid_send, mid_recv, d, mid_peer))
        nears.append(pass_on(slot, near_send, near_recv, d, near_peer))
        from_mid(d - 1)
    from_mid(hops - 1)
    for copy in nears + later:
        copy.wait_recv()
    sent += fars[1:] + mids + nears + later

    total = shards * rows
    peak[...] = jnp.full_like(peak, -jnp.inf)
    mass[...] = jnp.zeros_like(mass)
    picked[...] = jnp.zeros_like(picked)
    first = me * (tiles * tile)

    def score_tile(i, carry):
        fetch(i).wait()
        everyone = rows_all[...].reshape(total, rows_all.shape[2])
        logits = jnp.dot(everyone, weight_all[i], preferred_element_type=F32)
        ids = meta_all[:, :rows, :].reshape(total, LANES)
        parts = [logits[:, p * LANES : (p + 1) * LANES] for p in range(tile // LANES)]
        old = peak[...]
        new = functools.reduce(jnp.maximum, parts, old)
        add = mass[...] * jnp.exp(old - new)
        pick = picked[...]
        lane = lax.broadcasted_iota(jnp.int32, (total, LANES), 1) - ids
        for p, part in enumerate(parts):
            add = add + jnp.exp(part - new)
            pick = pick + jnp.where(lane == -(first + i * tile + p * LANES), part, 0.0)
        peak[...] = new
        mass[...] = add
        picked[...] = pick
        return carry

    lax.fori_loop(0, tiles, score_tile, 0)
    top = jnp.max(peak[...], 1, keepdims=True)
    summed = jnp.sum(mass[...] * jnp.exp(peak[...] - top), 1, keepdims=True)
    chosen = jnp.sum(picked[...], 1, keepdims=True)
    lane = lax.broadcasted_iota(jnp.int32, (total, LANES), 1)
    packed = jnp.where(lane == 0, top, jnp.where(lane == 1, summed, chosen))
    stats[...] = packed.reshape(shards, rows, LANES)

    arriving = []
    for k in range(1, shards):
        dest = lax.rem(me + k, shards)
        arriving.append(
            send(stats.at[dest], stats_all.at[me], stat_send.at[k], stat_recv.at[k], dest)
        )
    stats_all[me] = stats[me]
    for copy in arriving:
        copy.wait_recv()
    sent += arriving
    tops = stats_all[:, :, 0:1]
    overall = jnp.max(tops, 0)
    masses = jnp.sum(stats_all[:, :, 1:2] * jnp.exp(tops - overall[None]), 0)
    logprob = jnp.sum(stats_all[:, :, 2:3], 0) - (overall + jnp.log(masses))
    logprob = jnp.broadcast_to(logprob, (rows, LANES))
    slots = rows // choice_lengths.shape[1]
    spot = lax.broadcasted_iota(jnp.int32, (slots, LANES), 0)
    for c in range(choice_lengths.shape[1]):
        count = choice_lengths[0, c]
        mine = jnp.where(spot < count, logprob[c * slots : (c + 1) * slots], 0.0)
        scores[c : c + 1, :] = jnp.sum(mine, 0, keepdims=True) / jnp.full(
            (1, LANES), count, jnp.int32
        ).astype(F32)
    for copy in sent:
        copy.wait_send()


VMEM = pl.BlockSpec(memory_space=pltpu.VMEM)
SMEM = pl.BlockSpec(memory_space=pltpu.SMEM)


def local(*args):
    prefix, answers = args[:5], args[5:11]
    doc_lengths, question_doc, choice_tokens, choice_lengths, head_weight = args[11:]
    shards = lax.axis_size("seq")
    my_index = lax.axis_index("seq")
    tok_rows, width = prefix[0].shape
    answers = [a.reshape(-1, width) for a in answers]
    rows = answers[0].shape[0]
    units = width // LANES
    copies = max(shards // units, 1)
    block = 2 * WIDE

    moves, pulled, fresh = pl.pallas_call(
        states_kernel,
        grid=(width // block,),
        in_specs=[pl.BlockSpec((tok_rows, block), lambda i: (0, i))] * 5
        + [pl.BlockSpec((rows, block), lambda i: (0, i))] * 6,
        out_specs=[
            pl.BlockSpec((block // LANES, LANES, LANES), lambda i: (i, 0, 0)),
            pl.BlockSpec((rows, block), lambda i: (0, i)),
            pl.BlockSpec((rows, block), lambda i: (0, i)),
        ],
        out_shape=[
            jax.ShapeDtypeStruct((units, LANES, LANES), F32),
            jax.ShapeDtypeStruct((rows, width), F32),
            jax.ShapeDtypeStruct((rows, width), F32),
        ],
        compiler_params=pltpu.CompilerParams(vmem_limit_bytes=60 * 2**20),
        name="states",
    )(*prefix, *answers)
    meta = jnp.concatenate(
        [choice_tokens.reshape(-1), jnp.broadcast_to(question_doc, (8,))]
    )
    meta = jnp.broadcast_to(meta[:, None], (rows + 8, LANES))
    vocab_dev = head_weight.shape[1]
    tile = 512
    all_rows = shards * rows
    choices = choice_tokens.shape[1]
    dma = pltpu.SemaphoreType.DMA
    scores = pl.pallas_call(
        functools.partial(score_kernel, copies),
        in_specs=[SMEM, SMEM, VMEM, VMEM, VMEM, VMEM, pl.BlockSpec(memory_space=pl.ANY)],
        out_specs=VMEM,
        out_shape=jax.ShapeDtypeStruct((choices, LANES), F32),
        scratch_shapes=[
            pltpu.VMEM((shards, rows + 8, LANES), jnp.int32),
            pltpu.VMEM((shards, LANES, LANES), F32),
            pltpu.VMEM((shards, HSIZE, LANES), BF16),
            pltpu.VMEM((units, HSIZE, LANES), BF16),
            pltpu.VMEM((shards, rows, width), BF16),
            pltpu.VMEM((vocab_dev // tile, width, tile), BF16),
            pltpu.VMEM((shards, rows, LANES), F32),
            pltpu.VMEM((shards, rows, LANES), F32),
            pltpu.VMEM((all_rows, LANES), F32),
            pltpu.VMEM((all_rows, LANES), F32),
            pltpu.VMEM((all_rows, LANES), F32),
            dma((vocab_dev // tile,)),
        ]
        + [dma((shards,))] * 14,
        compiler_params=pltpu.CompilerParams(
            vmem_limit_bytes=60 * 2**20, collective_id=0, has_side_effects=True
        ),
        name="score",
    )(doc_lengths, choice_lengths, meta, moves, pulled, fresh, head_weight)
    return scores[:, 0][None]


def solution(mesh):
    token = P(("group", "seq"), None)
    choice = P(("group", "seq"), None, None, None)
    placed = (token,) * 5 + (choice,) * 6
    placed += (
        P("group"),
        P(("group", "seq")),
        P(("group", "seq"), None, None),
        P(("group", "seq"), None),
        P(None, "seq"),
    )
    return jax.shard_map(
        local, mesh=mesh, in_specs=placed, out_specs=P(("group", "seq"), None), check_vma=False
    )
```

```python
import functools

import jax
import jax.numpy as jnp
from jax import lax
from jax.experimental import pallas as pl
from jax.experimental.pallas import tpu as pltpu
from jax.sharding import PartitionSpec as P

HSIZE = 64
LANES = 128
WIDE = 256
F32 = jnp.float32
BF16 = jnp.bfloat16


def split(x):
    high = x.astype(BF16)
    return high, (x - high.astype(F32)).astype(BF16)


def mm(a, b, dims):
    return lax.dot_general(a, b, (dims, ((), ())), preferred_element_type=F32)


NN = ((1,), (0,))
TN = ((0,), (0,))
NT = ((1,), (1,))


def dot3(a, b, dims=NN):
    ah, al = split(a)
    bh, bl = split(b)
    rows = a.shape[0]
    if dims != TN and rows % 16 == 0:
        both = mm(jnp.concatenate([ah, al], 0), bh, dims)
        return both[:rows] + (both[rows:] + mm(ah, bl, dims))
    return mm(ah, bh, dims) + (mm(al, bh, dims) + mm(ah, bl, dims))


def block_mask(rows, cols):
    return (
        lax.broadcasted_iota(jnp.int32, (rows, cols), 0) // HSIZE
        == lax.broadcasted_iota(jnp.int32, (rows, cols), 1) // HSIZE
    )


def head_sum(x, ones):
    rows = x.shape[0]
    high, low = split(x)
    both = mm(jnp.concatenate([high, low], 0), ones, NN)
    return both[:rows] + both[rows:]


def stack_heads(x):
    heads = x.shape[1] // HSIZE
    lane = lax.broadcasted_iota(jnp.int32, x.shape, 1) // HSIZE
    return jnp.concatenate([jnp.where(lane == h, x, jnp.zeros_like(x)) for h in range(heads)], 0)


def fold_heads(x):
    heads = x.shape[1] // HSIZE
    out = x[:HSIZE]
    for h in range(1, heads):
        out = out + x[h * HSIZE : (h + 1) * HSIZE]
    return out


def factors(kappa, decay, learn, ones):
    kappa = kappa.astype(F32)
    unit = kappa * lax.rsqrt(head_sum(kappa * kappa, ones) + 1e-06)
    return jnp.exp(-decay.astype(F32)), unit, unit * learn.astype(F32)


def stack_split(x):
    heads = x.shape[1] // HSIZE
    lane = lax.broadcasted_iota(jnp.int32, (1, x.shape[1]), 1) // HSIZE
    keep = [jnp.where(lane == h, 1.0, 0.0).astype(BF16) for h in range(heads)]
    return [jnp.concatenate([part * k for k in keep], 0) for part in split(x)]


def dot_stacked(a, stacked, dims):
    rows = a.shape[0]
    both = mm(jnp.concatenate(split(a), 0), stacked[0], dims)
    return both[:rows] + (both[rows:] + mm(a.astype(BF16), stacked[1], dims))


def merge(gain, pulled, faded, keys, size):
    rows, wide = pulled.shape
    pairs = rows // (2 * size)
    half = rows // 2

    def parted(x):
        x = x.reshape(pairs, 2, size, wide)
        return x[:, 0].reshape(half, wide), x[:, 1].reshape(half, wide)

    def joined(x, y):
        shape = (pairs, 1, size, wide)
        return jnp.concatenate([x.reshape(shape), y.reshape(shape)], 1).reshape(rows, wide)

    def scaled(x, by):
        return (x.reshape(pairs, size, wide) * by).reshape(half, wide)

    gain = gain.reshape(pairs, 2, 1, wide)
    gain_a, gain_b = gain[:, 0], gain[:, 1]
    pulled_a, pulled_b = parted(pulled)
    faded_a, faded_b = parted(faded)
    keys_a, keys_b = parted(keys)
    across = (half, half * (wide // HSIZE))
    same = (
        lax.broadcasted_iota(jnp.int32, across, 0) // size
        == lax.broadcasted_iota(jnp.int32, across, 1) % half // size
    )
    seen = jnp.where(same, dot_stacked(pulled_b, stack_split(faded_a), NT), 0.0)
    moved = scaled(pulled_b, gain_a) - dot_stacked(seen, stack_split(pulled_a), NN)
    hit = jnp.where(same, dot_stacked(keys_a, stack_split(pulled_b), NT), 0.0)
    kept = scaled(keys_a, gain_b) - dot_stacked(hit, stack_split(faded_b), NN)
    return (
        gain_a * gain_b,
        joined(pulled_a, moved),
        joined(scaled(faded_a, gain_b), faded_b),
        joined(kept, keys_b),
    )


def state_group(prefix, answers, ones, diag_block):
    key, value, kappa, decay, learn = prefix
    query, akey, avalue, akappa, adecay, alearn = answers
    rows, wide = key.shape
    arows = query.shape[0]
    retain, unit, removal = factors(
        jnp.concatenate([kappa, akappa], 0),
        jnp.concatenate([decay, adecay], 0),
        jnp.concatenate([learn, alearn], 0),
        ones,
    )

    def tiled(x):
        return x.reshape(-1, 8, wide)

    tiles = rows // 8
    aretain, aunit, aremoval = [tiled(x[rows:]) for x in (retain, unit, removal)]
    retain, unit, removal = [tiled(x[:rows]) for x in (retain, unit, removal)]
    akey, avalue = tiled(akey.astype(F32)), tiled(avalue.astype(F32))
    sub = lax.broadcasted_iota(jnp.int32, (tiles, 8, wide), 1)
    asub = sub[: arows // 8]
    pushed = tiled(key.astype(F32))
    pulled = unit
    apulled = tiled(query.astype(F32))
    out = jnp.zeros_like(apulled)
    for t in range(8):
        j = 7 - t
        pt = slice(t, t + 1)
        aj = slice(j, j + 1)
        terms = [apulled * akey[:, aj], apulled * aremoval[:, aj]]
        if t == 0:
            terms = [x.reshape(-1, wide) for x in terms]
            sums = head_sum(jnp.concatenate(terms, 0), ones)
            got, gone = tiled(sums[:arows]), tiled(sums[arows:])
        if t > 0:
            pj = slice(7 - t, 8 - t)
            terms = [pushed * unit[:, pt], pulled * removal[:, pj]] + terms
            terms = [x.reshape(-1, wide) for x in terms]
            sums = head_sum(jnp.concatenate(terms, 0), ones)
            new = pushed * retain[:, pt] - tiled(sums[:rows]) * removal[:, pt]
            pushed = jnp.where(sub < t, new, pushed)
            new = pulled * retain[:, pj] - tiled(sums[rows : 2 * rows]) * unit[:, pj]
            pulled = jnp.where(sub > 7 - t, new, pulled)
            got = tiled(sums[2 * rows : 2 * rows + arows])
            gone = tiled(sums[2 * rows + arows :])
        live = asub >= j
        out = out + jnp.where(live, got * avalue[:, aj], 0.0)
        apulled = jnp.where(live, apulled * aretain[:, aj] - gone * aunit[:, aj], apulled)
    gain = jnp.ones((tiles, 1, wide), F32)
    faded = removal
    for t in range(7, -1, -1):
        faded = jnp.where(sub == t, removal * gain, faded)
        gain = gain * retain[:, t : t + 1]
    pulled, faded, keys = [x.reshape(rows, wide) for x in (pulled, faded, pushed)]
    size = 8
    while size < rows:
        gain, pulled, faded, keys = merge(gain, pulled, faded, keys, size)
        size *= 2
    gain = gain.reshape(1, wide)
    low_rank = fold_heads(jnp.where(diag_block, dot3(pulled, faded, TN), 0.0))
    eye = (
        lax.broadcasted_iota(jnp.int32, (HSIZE, wide), 0)
        == lax.broadcasted_iota(jnp.int32, (HSIZE, wide), 1) % HSIZE
    )
    passage = jnp.where(eye, gain, 0.0) - low_rank
    high, low = split(keys)
    outer = mm(value, high, TN) + mm(value, low, TN)
    update = fold_heads(jnp.where(diag_block, outer, 0.0))
    return passage, update, apulled.reshape(arows, wide), out.reshape(arows, wide)


def states_kernel(*refs):
    pk, pv, pc, pd, pe, aq, ak, av, ac, ad, ae, moves, pulled, fresh = refs
    wide = WIDE
    diag_block = block_mask(wide, wide)
    ones = jnp.where(diag_block, 1.0, 0.0).astype(BF16)
    for g in range(pk.shape[1] // wide):
        s = slice(g * wide, (g + 1) * wide)
        passage, update, q, o = state_group(
            [r[:, s] for r in (pk, pv, pc, pd, pe)],
            [r[:, s] for r in (aq, ak, av, ac, ad, ae)],
            ones,
            diag_block,
        )
        for u in range(wide // LANES):
            lanes = slice(u * LANES, (u + 1) * LANES)
            moves[g * (wide // LANES) + u, :HSIZE] = passage[:, lanes]
            moves[g * (wide // LANES) + u, HSIZE:] = update[:, lanes]
        pulled[:, s] = q
        fresh[:, s] = o


def documents(lengths, moves):
    shards = moves.shape[0]
    docs = lengths.shape[0]
    starts = []
    total = jnp.int32(0)
    for d in range(docs):
        starts.append(total)
        total = total + lengths[d]
    now = [moves[jnp.minimum(starts[d], shards - 1), HSIZE:] for d in range(docs)]

    def step(j, now):
        out = []
        for d in range(docs):
            at = jnp.minimum(starts[d] + j, shards - 1)
            new = dot3(now[d], stack_heads(moves[at, :HSIZE])) + moves[at, HSIZE:]
            out.append(jnp.where(j < lengths[d], new, now[d]))
        return out

    return [x.astype(BF16) for x in lax.fori_loop(1, shards // 2, step, now)]


def hidden_unit(state, x, fresh, ones):
    memory = stack_heads(state.astype(F32)).astype(BF16)
    high, low = split(x)
    lowest = (x - high.astype(F32) - low.astype(F32)).astype(BF16)
    out = mm(high, memory, NT) + (mm(low, memory, NT) + mm(lowest, memory, NT)) + fresh
    centre = out - head_sum(out, ones) * (1.0 / HSIZE)
    spread = head_sum(centre * centre, ones) * (1.0 / HSIZE)
    return (centre * lax.rsqrt(spread + 1e-05)).astype(BF16)


def score_kernel(
    copies,
    lengths,
    choice_lengths,
    meta,
    moves,
    pulled,
    fresh,
    weight,
    scores,
    meta_all,
    moves_all,
    stage,
    state,
    rows_all,
    weight_all,
    stats,
    stats_all,
    peak,
    mass,
    picked,
    weight_sem,
    meta_send,
    meta_recv,
    move_send,
    move_recv,
    state_send,
    state_recv,
    far_send,
    far_recv,
    mid_send,
    mid_recv,
    near_send,
    near_recv,
    stat_send,
    stat_recv,
):
    shards = moves_all.shape[0]
    me = lax.axis_index("seq")
    rows = pulled.shape[0]
    tiles, _, tile = weight_all.shape

    def fetch(i):
        return pltpu.make_async_copy(
            weight.at[:, pl.ds(i * tile, tile)], weight_all.at[i], weight_sem.at[i]
        )

    for i in range(tiles):
        fetch(i).start()

    def send(source, target, send_sem, recv_sem, dest):
        copy = pltpu.make_async_remote_copy(
            src_ref=source,
            dst_ref=target,
            send_sem=send_sem,
            recv_sem=recv_sem,
            device_id={"seq": dest},
            device_id_type=pl.DeviceIdType.MESH,
        )
        copy.start()
        return copy

    barrier = pltpu.get_barrier_semaphore()
    for k in range(1, shards):
        pl.semaphore_signal(
            barrier,
            inc=1,
            device_id={"seq": lax.rem(me + k, shards)},
            device_id_type=pl.DeviceIdType.MESH,
        )
    pl.semaphore_wait(barrier, shards - 1)

    sent = []
    arriving = []
    for k in range(1, shards):
        dest = lax.rem(me + k, shards)
        small = send(meta, meta_all.at[me], meta_send.at[k], meta_recv.at[k], dest)
        large = send(
            moves.at[dest // copies], moves_all.at[me], move_send.at[k], move_recv.at[k], dest
        )
        arriving += [small, large]
    meta_all[me] = meta[...]
    moves_all[me] = moves[me // copies]
    for copy in arriving:
        copy.wait_recv()
    sent += arriving

    docs = documents(lengths, moves_all)
    for q in range(shards):
        asked = jnp.broadcast_to(meta_all[q, rows : rows + 1, :], docs[0].shape)
        chosen = docs[0].astype(F32)
        for d in range(1, len(docs)):
            chosen = jnp.where(asked == d, docs[d].astype(F32), chosen)
        stage[q] = chosen.astype(BF16)
    unit = me // copies
    arriving = []
    for k in range(copies, shards, copies):
        dest = lax.rem(me + k, shards)
        arriving.append(
            send(stage.at[dest], state.at[unit], state_send.at[k], state_recv.at[k], dest)
        )
    state[unit] = stage[me]
    for copy in arriving:
        copy.wait_recv()
    sent += arriving

    ones = jnp.where(block_mask(LANES, LANES), 1.0, 0.0).astype(BF16)
    for u in range(state.shape[0]):
        s = slice(u * LANES, (u + 1) * LANES)
        rows_all[me, :, s] = hidden_unit(state[u], pulled[:, s], fresh[:, s], ones)

    hops = shards // 4
    far, place = me // 4, lax.rem(me, 4)
    mid_peer = me + 2 - 4 * (place // 2)
    near_peer = me + 1 - 2 * lax.rem(me, 2)

    def pass_on(slot, send_sems, recv_sems, k, dest):
        return send(rows_all.at[slot], rows_all.at[slot], send_sems.at[k], recv_sems.at[k], dest)

    fars = [None]
    for d in range(1, hops):
        dest = lax.rem(far + d, hops) * 4 + place
        fars.append(pass_on(me, far_send, far_recv, d, dest))
    mids = [pass_on(me, mid_send, mid_recv, 0, mid_peer)]
    nears = [pass_on(me, near_send, near_recv, 0, near_peer)]
    later = []

    def from_mid(d):
        mids[d].wait_recv()
        slot = lax.rem(far - d + hops, hops) * 4 + lax.rem(place + 2, 4)
        later.append(pass_on(slot, near_send, near_recv, hops + d, near_peer))

    for d in range(1, hops):
        fars[d].wait_recv()
        slot = lax.rem(far - d + hops, hops) * 4 + place
        mids.append(pass_on(slot, mid_send, mid_recv, d, mid_peer))
        nears.append(pass_on(slot, near_send, near_recv, d, near_peer))
        from_mid(d - 1)
    from_mid(hops - 1)
    for copy in nears + later:
        copy.wait_recv()
    sent += fars[1:] + mids + nears + later

    total = shards * rows
    peak[...] = jnp.full_like(peak, -jnp.inf)
    mass[...] = jnp.zeros_like(mass)
    picked[...] = jnp.zeros_like(picked)
    first = me * (tiles * tile)

    def score_tile(i, carry):
        fetch(i).wait()
        everyone = rows_all[...].reshape(total, rows_all.shape[2])
        logits = jnp.dot(everyone, weight_all[i], preferred_element_type=F32)
        ids = meta_all[:, :rows, :].reshape(total, LANES)
        parts = [logits[:, p * LANES : (p + 1) * LANES] for p in range(tile // LANES)]
        old = peak[...]
        new = functools.reduce(jnp.maximum, parts, old)
        add = mass[...] * jnp.exp(old - new)
        pick = picked[...]
        lane = lax.broadcasted_iota(jnp.int32, (total, LANES), 1) - ids
        for p, part in enumerate(parts):
            add = add + jnp.exp(part - new)
            pick = pick + jnp.where(lane == -(first + i * tile + p * LANES), part, 0.0)
        peak[...] = new
        mass[...] = add
        picked[...] = pick
        return carry

    lax.fori_loop(0, tiles, score_tile, 0)
    top = jnp.max(peak[...], 1, keepdims=True)
    summed = jnp.sum(mass[...] * jnp.exp(peak[...] - top), 1, keepdims=True)
    chosen = jnp.sum(picked[...], 1, keepdims=True)
    lane = lax.broadcasted_iota(jnp.int32, (total, LANES), 1)
    packed = jnp.where(lane == 0, top, jnp.where(lane == 1, summed, chosen))
    stats[...] = packed.reshape(shards, rows, LANES)

    arriving = []
    for k in range(1, shards):
        dest = lax.rem(me + k, shards)
        arriving.append(
            send(stats.at[dest], stats_all.at[me], stat_send.at[k], stat_recv.at[k], dest)
        )
    stats_all[me] = stats[me]
    for copy in arriving:
        copy.wait_recv()
    sent += arriving
    tops = stats_all[:, :, 0:1]
    overall = jnp.max(tops, 0)
    masses = jnp.sum(stats_all[:, :, 1:2] * jnp.exp(tops - overall[None]), 0)
    logprob = jnp.sum(stats_all[:, :, 2:3], 0) - (overall + jnp.log(masses))
    logprob = jnp.broadcast_to(logprob, (rows, LANES))
    slots = rows // choice_lengths.shape[1]
    spot = lax.broadcasted_iota(jnp.int32, (slots, LANES), 0)
    for c in range(choice_lengths.shape[1]):
        count = choice_lengths[0, c]
        mine = jnp.where(spot < count, logprob[c * slots : (c + 1) * slots], 0.0)
        scores[c : c + 1, :] = jnp.sum(mine, 0, keepdims=True) / jnp.full(
            (1, LANES), count, jnp.int32
        ).astype(F32)
    for copy in sent:
        copy.wait_send()


VMEM = pl.BlockSpec(memory_space=pltpu.VMEM)
SMEM = pl.BlockSpec(memory_space=pltpu.SMEM)


def local(*args):
    prefix, answers = args[:5], args[5:11]
    doc_lengths, question_doc, choice_tokens, choice_lengths, head_weight = args[11:]
    shards = lax.axis_size("seq")
    my_index = lax.axis_index("seq")
    tok_rows, width = prefix[0].shape
    answers = [a.reshape(-1, width) for a in answers]
    rows = answers[0].shape[0]
    units = width // LANES
    copies = max(shards // units, 1)
    block = 2 * WIDE

    moves, pulled, fresh = pl.pallas_call(
        states_kernel,
        grid=(width // block,),
        in_specs=[pl.BlockSpec((tok_rows, block), lambda i: (0, i))] * 5
        + [pl.BlockSpec((rows, block), lambda i: (0, i))] * 6,
        out_specs=[
            pl.BlockSpec((block // LANES, LANES, LANES), lambda i: (i, 0, 0)),
            pl.BlockSpec((rows, block), lambda i: (0, i)),
            pl.BlockSpec((rows, block), lambda i: (0, i)),
        ],
        out_shape=[
            jax.ShapeDtypeStruct((units, LANES, LANES), F32),
            jax.ShapeDtypeStruct((rows, width), F32),
            jax.ShapeDtypeStruct((rows, width), F32),
        ],
        compiler_params=pltpu.CompilerParams(vmem_limit_bytes=60 * 2**20),
        name="states",
    )(*prefix, *answers)
    meta = jnp.concatenate(
        [choice_tokens.reshape(-1), jnp.broadcast_to(question_doc, (8,))]
    )
    meta = jnp.broadcast_to(meta[:, None], (rows + 8, LANES))
    vocab_dev = head_weight.shape[1]
    tile = 512
    all_rows = shards * rows
    choices = choice_tokens.shape[1]
    dma = pltpu.SemaphoreType.DMA
    scores = pl.pallas_call(
        functools.partial(score_kernel, copies),
        in_specs=[SMEM, SMEM, VMEM, VMEM, VMEM, VMEM, pl.BlockSpec(memory_space=pl.ANY)],
        out_specs=VMEM,
        out_shape=jax.ShapeDtypeStruct((choices, LANES), F32),
        scratch_shapes=[
            pltpu.VMEM((shards, rows + 8, LANES), jnp.int32),
            pltpu.VMEM((shards, LANES, LANES), F32),
            pltpu.VMEM((shards, HSIZE, LANES), BF16),
            pltpu.VMEM((units, HSIZE, LANES), BF16),
            pltpu.VMEM((shards, rows, width), BF16),
            pltpu.VMEM((vocab_dev // tile, width, tile), BF16),
            pltpu.VMEM((shards, rows, LANES), F32),
            pltpu.VMEM((shards, rows, LANES), F32),
            pltpu.VMEM((all_rows, LANES), F32),
            pltpu.VMEM((all_rows, LANES), F32),
            pltpu.VMEM((all_rows, LANES), F32),
            dma((vocab_dev // tile,)),
        ]
        + [dma((shards,))] * 14,
        compiler_params=pltpu.CompilerParams(
            vmem_limit_bytes=60 * 2**20, collective_id=0, has_side_effects=True
        ),
        name="score",
    )(doc_lengths, choice_lengths, meta, moves, pulled, fresh, head_weight)
    return scores[:, 0][None]


def solution(mesh):
    token = P(("group", "seq"), None)
    choice = P(("group", "seq"), None, None, None)
    placed = (token,) * 5 + (choice,) * 6
    placed += (
        P("group"),
        P(("group", "seq")),
        P(("group", "seq"), None, None),
        P(("group", "seq"), None),
        P(None, "seq"),
    )
    return jax.shard_map(
        local, mesh=mesh, in_specs=placed, out_specs=P(("group", "seq"), None), check_vma=False
    )
```

```python
import functools

import jax
import jax.numpy as jnp
from jax import lax
from jax.experimental import pallas as pl
from jax.experimental.pallas import tpu as pltpu
from jax.sharding import PartitionSpec as P

HSIZE = 64
LANES = 128
WIDE = 256
F32 = jnp.float32
BF16 = jnp.bfloat16


def split(x):
    high = x.astype(BF16)
    return high, (x - high.astype(F32)).astype(BF16)


def mm(a, b, dims):
    return lax.dot_general(a, b, (dims, ((), ())), preferred_element_type=F32)


NN = ((1,), (0,))
TN = ((0,), (0,))
NT = ((1,), (1,))


def dot3(a, b, dims=NN):
    ah, al = split(a)
    bh, bl = split(b)
    rows = a.shape[0]
    if dims != TN and rows % 16 == 0:
        both = mm(jnp.concatenate([ah, al], 0), bh, dims)
        return both[:rows] + (both[rows:] + mm(ah, bl, dims))
    return mm(ah, bh, dims) + (mm(al, bh, dims) + mm(ah, bl, dims))


def block_mask(rows, cols):
    return (
        lax.broadcasted_iota(jnp.int32, (rows, cols), 0) // HSIZE
        == lax.broadcasted_iota(jnp.int32, (rows, cols), 1) // HSIZE
    )


def head_sum(x, ones):
    rows = x.shape[0]
    high, low = split(x)
    both = mm(jnp.concatenate([high, low], 0), ones, NN)
    return both[:rows] + both[rows:]


def stack_heads(x):
    heads = x.shape[1] // HSIZE
    lane = lax.broadcasted_iota(jnp.int32, x.shape, 1) // HSIZE
    return jnp.concatenate([jnp.where(lane == h, x, jnp.zeros_like(x)) for h in range(heads)], 0)


def fold_heads(x):
    heads = x.shape[1] // HSIZE
    out = x[:HSIZE]
    for h in range(1, heads):
        out = out + x[h * HSIZE : (h + 1) * HSIZE]
    return out


def factors(kappa, decay, learn, ones):
    kappa = kappa.astype(F32)
    unit = kappa * lax.rsqrt(head_sum(kappa * kappa, ones) + 1e-06)
    return jnp.exp(-decay.astype(F32)), unit, unit * learn.astype(F32)


def stack_split(x):
    heads = x.shape[1] // HSIZE
    lane = lax.broadcasted_iota(jnp.int32, (1, x.shape[1]), 1) // HSIZE
    keep = [jnp.where(lane == h, 1.0, 0.0).astype(BF16) for h in range(heads)]
    return [jnp.concatenate([part * k for k in keep], 0) for part in split(x)]


def dot_stacked(a, stacked, dims):
    rows = a.shape[0]
    both = mm(jnp.concatenate(split(a), 0), stacked[0], dims)
    return both[:rows] + (both[rows:] + mm(a.astype(BF16), stacked[1], dims))


def merge(gain, pulled, faded, keys, size):
    rows, wide = pulled.shape
    pairs = rows // (2 * size)
    half = rows // 2

    def parted(x):
        x = x.reshape(pairs, 2, size, wide)
        return x[:, 0].reshape(half, wide), x[:, 1].reshape(half, wide)

    def joined(x, y):
        shape = (pairs, 1, size, wide)
        return jnp.concatenate([x.reshape(shape), y.reshape(shape)], 1).reshape(rows, wide)

    def scaled(x, by):
        return (x.reshape(pairs, size, wide) * by).reshape(half, wide)

    gain = gain.reshape(pairs, 2, 1, wide)
    gain_a, gain_b = gain[:, 0], gain[:, 1]
    pulled_a, pulled_b = parted(pulled)
    faded_a, faded_b = parted(faded)
    keys_a, keys_b = parted(keys)
    across = (half, half * (wide // HSIZE))
    same = (
        lax.broadcasted_iota(jnp.int32, across, 0) // size
        == lax.broadcasted_iota(jnp.int32, across, 1) % half // size
    )
    seen = jnp.where(same, dot_stacked(pulled_b, stack_split(faded_a), NT), 0.0)
    moved = scaled(pulled_b, gain_a) - dot_stacked(seen, stack_split(pulled_a), NN)
    hit = jnp.where(same, dot_stacked(keys_a, stack_split(pulled_b), NT), 0.0)
    kept = scaled(keys_a, gain_b) - dot_stacked(hit, stack_split(faded_b), NN)
    return (
        gain_a * gain_b,
        joined(pulled_a, moved),
        joined(scaled(faded_a, gain_b), faded_b),
        joined(kept, keys_b),
    )


def state_group(prefix, answers, ones, diag_block):
    key, value, kappa, decay, learn = prefix
    query, akey, avalue, akappa, adecay, alearn = answers
    rows, wide = key.shape
    arows = query.shape[0]
    retain, unit, removal = factors(
        jnp.concatenate([kappa, akappa], 0),
        jnp.concatenate([decay, adecay], 0),
        jnp.concatenate([learn, alearn], 0),
        ones,
    )

    def tiled(x):
        return x.reshape(-1, 8, wide)

    tiles = rows // 8
    aretain, aunit, aremoval = [tiled(x[rows:]) for x in (retain, unit, removal)]
    retain, unit, removal = [tiled(x[:rows]) for x in (retain, unit, removal)]
    akey, avalue = tiled(akey.astype(F32)), tiled(avalue.astype(F32))
    sub = lax.broadcasted_iota(jnp.int32, (tiles, 8, wide), 1)
    asub = sub[: arows // 8]
    pushed = tiled(key.astype(F32))
    pulled = unit
    apulled = tiled(query.astype(F32))
    out = jnp.zeros_like(apulled)
    for t in range(8):
        j = 7 - t
        pt = slice(t, t + 1)
        aj = slice(j, j + 1)
        terms = [apulled * akey[:, aj], apulled * aremoval[:, aj]]
        if t == 0:
            terms = [x.reshape(-1, wide) for x in terms]
            sums = head_sum(jnp.concatenate(terms, 0), ones)
            got, gone = tiled(sums[:arows]), tiled(sums[arows:])
        if t > 0:
            pj = slice(7 - t, 8 - t)
            terms = [pushed * unit[:, pt], pulled * removal[:, pj]] + terms
            terms = [x.reshape(-1, wide) for x in terms]
            sums = head_sum(jnp.concatenate(terms, 0), ones)
            new = pushed * retain[:, pt] - tiled(sums[:rows]) * removal[:, pt]
            pushed = jnp.where(sub < t, new, pushed)
            new = pulled * retain[:, pj] - tiled(sums[rows : 2 * rows]) * unit[:, pj]
            pulled = jnp.where(sub > 7 - t, new, pulled)
            got = tiled(sums[2 * rows : 2 * rows + arows])
            gone = tiled(sums[2 * rows + arows :])
        live = asub >= j
        out = out + jnp.where(live, got * avalue[:, aj], 0.0)
        apulled = jnp.where(live, apulled * aretain[:, aj] - gone * aunit[:, aj], apulled)
    gain = jnp.ones((tiles, 1, wide), F32)
    faded = removal
    for t in range(7, -1, -1):
        faded = jnp.where(sub == t, removal * gain, faded)
        gain = gain * retain[:, t : t + 1]
    pulled, faded, keys = [x.reshape(rows, wide) for x in (pulled, faded, pushed)]
    size = 8
    while size < rows:
        gain, pulled, faded, keys = merge(gain, pulled, faded, keys, size)
        size *= 2
    gain = gain.reshape(1, wide)
    low_rank = fold_heads(jnp.where(diag_block, dot3(pulled, faded, TN), 0.0))
    eye = (
        lax.broadcasted_iota(jnp.int32, (HSIZE, wide), 0)
        == lax.broadcasted_iota(jnp.int32, (HSIZE, wide), 1) % HSIZE
    )
    passage = jnp.where(eye, gain, 0.0) - low_rank
    high, low = split(keys)
    outer = mm(value, high, TN) + mm(value, low, TN)
    update = fold_heads(jnp.where(diag_block, outer, 0.0))
    return passage, update, apulled.reshape(arows, wide), out.reshape(arows, wide)


def documents(lengths, moves):
    shards = moves.shape[0]
    docs = lengths.shape[0]
    starts = []
    total = jnp.int32(0)
    for d in range(docs):
        starts.append(total)
        total = total + lengths[d]
    now = [moves[jnp.minimum(starts[d], shards - 1), HSIZE:] for d in range(docs)]

    def step(j, now):
        out = []
        for d in range(docs):
            at = jnp.minimum(starts[d] + j, shards - 1)
            new = dot3(now[d], stack_heads(moves[at, :HSIZE])) + moves[at, HSIZE:]
            out.append(jnp.where(j < lengths[d], new, now[d]))
        return out

    return [x.astype(BF16) for x in lax.fori_loop(1, shards // 2, step, now)]


def hidden_unit(state, x, fresh, ones):
    memory = stack_heads(state.astype(F32)).astype(BF16)
    high, low = split(x)
    lowest = (x - high.astype(F32) - low.astype(F32)).astype(BF16)
    out = mm(high, memory, NT) + (mm(low, memory, NT) + mm(lowest, memory, NT)) + fresh
    centre = out - head_sum(out, ones) * (1.0 / HSIZE)
    spread = head_sum(centre * centre, ones) * (1.0 / HSIZE)
    return (centre * lax.rsqrt(spread + 1e-05)).astype(BF16)


def score_kernel(
    copies,
    lengths,
    choice_lengths,
    meta,
    *refs,
):
    (
        prefix,
        answers,
        weight,
        scores,
        moves,
        pulled,
        fresh,
        meta_all,
        moves_all,
        stage,
        state,
        rows_all,
        weight_all,
        stats,
        stats_all,
        peak,
        mass,
        picked,
        weight_sem,
        meta_send,
        meta_recv,
        move_send,
        move_recv,
        state_send,
        state_recv,
        far_send,
        far_recv,
        mid_send,
        mid_recv,
        near_send,
        near_recv,
        stat_send,
        stat_recv,
    ) = (refs[:5], refs[5:11]) + refs[11:]
    shards = moves_all.shape[0]
    me = lax.axis_index("seq")
    rows = pulled.shape[0]
    tiles, _, tile = weight_all.shape

    def fetch(i):
        return pltpu.make_async_copy(
            weight.at[:, pl.ds(i * tile, tile)], weight_all.at[i], weight_sem.at[i]
        )

    for i in range(tiles):
        fetch(i).start()

    def plan(source, target, send_sem, recv_sem, dest):
        return pltpu.make_async_remote_copy(
            src_ref=source,
            dst_ref=target,
            send_sem=send_sem,
            recv_sem=recv_sem,
            device_id={"seq": dest},
            device_id_type=pl.DeviceIdType.MESH,
        )

    def send(*route):
        copy = plan(*route)
        copy.start()
        return copy

    barrier = pltpu.get_barrier_semaphore()
    for k in range(1, shards):
        pl.semaphore_signal(
            barrier,
            inc=1,
            device_id={"seq": lax.rem(me + k, shards)},
            device_id_type=pl.DeviceIdType.MESH,
        )
    pl.semaphore_wait(barrier, shards - 1)

    sent = []
    arriving = []
    for k in range(1, shards):
        dest = lax.rem(me + k, shards)
        arriving.append(
            send(meta, meta_all.at[me], meta_send.at[k], meta_recv.at[k], dest)
        )
    meta_all[me] = meta[...]

    def move(unit, source, peer):
        return plan(
            moves.at[unit], moves_all.at[source], move_send.at[peer], move_recv.at[source], peer
        )

    diag_block = block_mask(WIDE, WIDE)
    wide_ones = jnp.where(diag_block, 1.0, 0.0).astype(BF16)
    per_group = WIDE // LANES

    def state_step(i, carry):
        for g in range(2):
            s = pl.ds(pl.multiple_of((i * 2 + g) * WIDE, WIDE), WIDE)
            passage, update, q, o = state_group(
                [r[:, s] for r in prefix], [r[:, s] for r in answers], wide_ones, diag_block
            )
            pulled[:, s] = q
            fresh[:, s] = o
            for u in range(per_group):
                lanes = slice(u * LANES, (u + 1) * LANES)
                unit = (i * 2 + g) * per_group + u
                moves[unit, :HSIZE] = passage[:, lanes]
                moves[unit, HSIZE:] = update[:, lanes]
        for u in range(2 * per_group):
            unit = i * (2 * per_group) + u
            for c in range(copies):
                peer = unit * copies + c

                @pl.when(peer != me)
                def _():
                    move(unit, me, peer).start()

        return carry

    lax.fori_loop(0, moves.shape[0] // (2 * per_group), state_step, 0)
    moves_all[me] = moves[me // copies]
    for copy in arriving:
        copy.wait_recv()
    for source in range(shards):

        @pl.when(source != me)
        def _():
            move(source // copies, source, source).wait_recv()

    sent += arriving

    docs = documents(lengths, moves_all)
    for q in range(shards):
        asked = jnp.broadcast_to(meta_all[q, rows : rows + 1, :], docs[0].shape)
        chosen = docs[0].astype(F32)
        for d in range(1, len(docs)):
            chosen = jnp.where(asked == d, docs[d].astype(F32), chosen)
        stage[q] = chosen.astype(BF16)
    unit = me // copies
    arriving = []
    for k in range(copies, shards, copies):
        dest = lax.rem(me + k, shards)
        arriving.append(
            send(stage.at[dest], state.at[unit], state_send.at[k], state_recv.at[k], dest)
        )
    state[unit] = stage[me]
    for copy in arriving:
        copy.wait_recv()
    sent += arriving

    ones = jnp.where(block_mask(LANES, LANES), 1.0, 0.0).astype(BF16)
    for u in range(state.shape[0]):
        s = slice(u * LANES, (u + 1) * LANES)
        rows_all[me, :, s] = hidden_unit(state[u], pulled[:, s], fresh[:, s], ones)

    hops = shards // 4
    far, place = me // 4, lax.rem(me, 4)
    mid_peer = me + 2 - 4 * (place // 2)
    near_peer = me + 1 - 2 * lax.rem(me, 2)

    def pass_on(slot, send_sems, recv_sems, k, dest):
        return send(rows_all.at[slot], rows_all.at[slot], send_sems.at[k], recv_sems.at[k], dest)

    fars = [None]
    for d in range(1, hops):
        dest = lax.rem(far + d, hops) * 4 + place
        fars.append(pass_on(me, far_send, far_recv, d, dest))
    mids = [pass_on(me, mid_send, mid_recv, 0, mid_peer)]
    nears = [pass_on(me, near_send, near_recv, 0, near_peer)]
    later = []

    def from_mid(d):
        mids[d].wait_recv()
        slot = lax.rem(far - d + hops, hops) * 4 + lax.rem(place + 2, 4)
        later.append(pass_on(slot, near_send, near_recv, hops + d, near_peer))

    for d in range(1, hops):
        fars[d].wait_recv()
        slot = lax.rem(far - d + hops, hops) * 4 + place
        mids.append(pass_on(slot, mid_send, mid_recv, d, mid_peer))
        nears.append(pass_on(slot, near_send, near_recv, d, near_peer))
        from_mid(d - 1)
    from_mid(hops - 1)
    for copy in nears + later:
        copy.wait_recv()
    sent += fars[1:] + mids + nears + later

    total = shards * rows
    peak[...] = jnp.full_like(peak, -jnp.inf)
    mass[...] = jnp.zeros_like(mass)
    picked[...] = jnp.zeros_like(picked)
    first = me * (tiles * tile)

    def score_tile(i, carry):
        fetch(i).wait()
        everyone = rows_all[...].reshape(total, rows_all.shape[2])
        logits = jnp.dot(everyone, weight_all[i], preferred_element_type=F32)
        ids = meta_all[:, :rows, :].reshape(total, LANES)
        parts = [logits[:, p * LANES : (p + 1) * LANES] for p in range(tile // LANES)]
        old = peak[...]
        new = functools.reduce(jnp.maximum, parts, old)
        add = mass[...] * jnp.exp(old - new)
        pick = picked[...]
        lane = lax.broadcasted_iota(jnp.int32, (total, LANES), 1) - ids
        for p, part in enumerate(parts):
            add = add + jnp.exp(part - new)
            pick = pick + jnp.where(lane == -(first + i * tile + p * LANES), part, 0.0)
        peak[...] = new
        mass[...] = add
        picked[...] = pick
        return carry

    lax.fori_loop(0, tiles, score_tile, 0)
    top = jnp.max(peak[...], 1, keepdims=True)
    summed = jnp.sum(mass[...] * jnp.exp(peak[...] - top), 1, keepdims=True)
    chosen = jnp.sum(picked[...], 1, keepdims=True)
    lane = lax.broadcasted_iota(jnp.int32, (total, LANES), 1)
    packed = jnp.where(lane == 0, top, jnp.where(lane == 1, summed, chosen))
    stats[...] = packed.reshape(shards, rows, LANES)

    arriving = []
    for k in range(1, shards):
        dest = lax.rem(me + k, shards)
        arriving.append(
            send(stats.at[dest], stats_all.at[me], stat_send.at[k], stat_recv.at[k], dest)
        )
    stats_all[me] = stats[me]
    for copy in arriving:
        copy.wait_recv()
    sent += arriving
    tops = stats_all[:, :, 0:1]
    overall = jnp.max(tops, 0)
    masses = jnp.sum(stats_all[:, :, 1:2] * jnp.exp(tops - overall[None]), 0)
    logprob = jnp.sum(stats_all[:, :, 2:3], 0) - (overall + jnp.log(masses))
    logprob = jnp.broadcast_to(logprob, (rows, LANES))
    slots = rows // choice_lengths.shape[1]
    spot = lax.broadcasted_iota(jnp.int32, (slots, LANES), 0)
    for c in range(choice_lengths.shape[1]):
        count = choice_lengths[0, c]
        mine = jnp.where(spot < count, logprob[c * slots : (c + 1) * slots], 0.0)
        scores[c : c + 1, :] = jnp.sum(mine, 0, keepdims=True) / jnp.full(
            (1, LANES), count, jnp.int32
        ).astype(F32)
    for copy in sent:
        copy.wait_send()
    for peer in range(shards):

        @pl.when(peer != me)
        def _():
            move(peer // copies, me, peer).wait_send()


VMEM = pl.BlockSpec(memory_space=pltpu.VMEM)
SMEM = pl.BlockSpec(memory_space=pltpu.SMEM)


def local(*args):
    prefix, answers = args[:5], args[5:11]
    doc_lengths, question_doc, choice_tokens, choice_lengths, head_weight = args[11:]
    shards = lax.axis_size("seq")
    my_index = lax.axis_index("seq")
    tok_rows, width = prefix[0].shape
    answers = [a.reshape(-1, width) for a in answers]
    rows = answers[0].shape[0]
    units = width // LANES
    copies = max(shards // units, 1)
    meta = jnp.concatenate(
        [choice_tokens.reshape(-1), jnp.broadcast_to(question_doc, (8,))]
    )
    meta = jnp.broadcast_to(meta[:, None], (rows + 8, LANES))
    vocab_dev = head_weight.shape[1]
    tile = 512
    all_rows = shards * rows
    choices = choice_tokens.shape[1]
    dma = pltpu.SemaphoreType.DMA
    scores = pl.pallas_call(
        functools.partial(score_kernel, copies),
        in_specs=[SMEM, SMEM] + [VMEM] * 12 + [pl.BlockSpec(memory_space=pl.ANY)],
        out_specs=VMEM,
        out_shape=jax.ShapeDtypeStruct((choices, LANES), F32),
        scratch_shapes=[
            pltpu.VMEM((units, LANES, LANES), F32),
            pltpu.VMEM((rows, width), F32),
            pltpu.VMEM((rows, width), F32),
            pltpu.VMEM((shards, rows + 8, LANES), jnp.int32),
            pltpu.VMEM((shards, LANES, LANES), F32),
            pltpu.VMEM((shards, HSIZE, LANES), BF16),
            pltpu.VMEM((units, HSIZE, LANES), BF16),
            pltpu.VMEM((shards, rows, width), BF16),
            pltpu.VMEM((vocab_dev // tile, width, tile), BF16),
            pltpu.VMEM((shards, rows, LANES), F32),
            pltpu.VMEM((shards, rows, LANES), F32),
            pltpu.VMEM((all_rows, LANES), F32),
            pltpu.VMEM((all_rows, LANES), F32),
            pltpu.VMEM((all_rows, LANES), F32),
            dma((vocab_dev // tile,)),
        ]
        + [dma((shards,))] * 14,
        compiler_params=pltpu.CompilerParams(
            vmem_limit_bytes=60 * 2**20, collective_id=0, has_side_effects=True
        ),
        name="score",
    )(doc_lengths, choice_lengths, meta, *prefix, *answers, head_weight)
    return scores[:, 0][None]


def solution(mesh):
    token = P(("group", "seq"), None)
    choice = P(("group", "seq"), None, None, None)
    placed = (token,) * 5 + (choice,) * 6
    placed += (
        P("group"),
        P(("group", "seq")),
        P(("group", "seq"), None, None),
        P(("group", "seq"), None),
        P(None, "seq"),
    )
    return jax.shard_map(
        local, mesh=mesh, in_specs=placed, out_specs=P(("group", "seq"), None), check_vma=False
    )
```
